32 devices in a mesh: groups: 2 (over y), ctx: 4 (over z), fsdp: 4 (over x, core).
Axes of the slice: x: 2, y: 2, z: 4, core: 2. Of those that a mesh axis runs over, the one named last changes fastest.
Arguments:
- patches: bfloat16 [8, 1024, 1024], P(('groups', 'fsdp'), 'ctx'), parts along dimension 0, may hold values from -6 to 6
- segment_ids: int32 [8, 1024], P(('groups', 'fsdp'), 'ctx'), parts along dimension 0, may hold values from 0 to 15, never falling along the last dimension, each value on 1 to 768 neighbouring positions
- patch_rows: int32 [8, 1024], P(('groups', 'fsdp'), 'ctx'), parts along dimension 0, may hold values from 0 to 63
- patch_cols: int32 [8, 1024], P(('groups', 'fsdp'), 'ctx'), parts along dimension 0, may hold values from 0 to 63
- row_table: bfloat16 [64, 1024], replicated, may hold values from -3 to 3
- col_table: bfloat16 [64, 1024], replicated, may hold values from -3 to 3
- norm_gain: float32 [1024], replicated, may hold values from 0.1 to 1.9
- qkv_weight: bfloat16 [1024, 3072], P('fsdp'), may hold values from -5 to 5
- out_weight: bfloat16 [1024, 1024], P(None, 'fsdp'), may hold values from -0.1875 to 0.1875
Outputs:
- encoded: bfloat16 [8, 1024, 1024], P(('groups', 'fsdp'), 'ctx'), parts along dimension 0
The draws below stay inside these ranges and needn't reach their ends.
There are 2 independent parts, one for each index of `groups`. The reference program is written for one: setup_inputs(seed, part) draws one part's arguments, and reference() takes and returns one part's arrays. A program takes and returns all parts, laid end to end along the dimension named above; an argument that names none is the same for every part. Nothing has to cross between parts.
All inputs are finite; a program needn't handle non-finite values.
Results may differ from the reference program's by a relative error of at most 0.0044.
The reference program's roundings to bfloat16 on the way count: a program that leaves them out, or rounds other values in their place, can miss the bound.
Values may be sent and summed in bfloat16 or wider, within the bound.
No kernel may reach another device: no remote copies, remote signals or barrier semaphores. Data moves between devices by JAX's collectives and lax.ppermute only.
A program may use at most 64 MiB of HBM per device.

```python
import math
import jax
import jax.numpy as jnp
import numpy as np
from jax import lax

D = 1024
HEADS = 16
GRID = 64
SEGS = 16
LEN = 1024
SEQS = 4
SEG_MOST = 768


def draw_qkv_weight(key, part):
    base = jnp.clip(jax.random.normal(key, (D, 3 * D), jnp.float32), -2.5, 2.5) * D ** (-0.5)
    return base.astype(jnp.bfloat16)


def touch_ends(entries, key, smallest, top_value):
    longest = entries.shape.index(max(entries.shape))
    spots = []
    for shift in (0, 1):
        where = [jax.random.randint(jax.random.fold_in(key, axis), (), 0, length) for axis, length in enumerate(entries.shape)]
        where[longest] = (where[longest] + shift) % entries.shape[longest]
        spots.append(tuple(where))
    return entries.at[spots[0]].set(smallest).at[spots[1]].set(top_value)


def levels(stream_key, extent, split, low, high):
    def one(dim, blocks):
        draws = jax.random.uniform(jax.random.fold_in(jax.random.fold_in(stream_key, 6), dim), (blocks,), jnp.float32, low / len(split), high / len(split))
        return jnp.repeat(jnp.exp(draws), extent[dim] // blocks).reshape((-1,) + (1,) * (len(extent) - dim - 1))

    level = one(*split[0])
    for cut in split[1:]:
        level = level * one(*cut)
    return level


def profile(amount, total, bound, lean):
    weights = [(1 << 20) // math.isqrt(rank ** lean) + 1 for rank in range(2, amount + 1)]
    spare, given = total - bound - (amount - 1), [1] * (amount - 1)
    while spare > 0:
        candidates = [i for i in range(amount - 1) if given[i] < bound]
        mass, budget = sum([weights[i] for i in candidates]), spare
        for i in candidates:
            addition = min(bound - given[i], max(1, budget * weights[i] // mass), spare)
            given[i] = given[i] + addition
            spare = spare - addition
    return np.array([bound] + given)


def ragged_sizes(own_key, amount, total, most, lean):
    if amount == 2:
        one = jax.random.randint(own_key, (), max(1, total - most), min(most, total - 1) + 1)
        return jnp.stack([one, total - one])
    tallies = jnp.asarray(profile(amount, total, most, lean), jnp.int32)
    pairs = (amount - 1) // 2
    donor, receiver = tallies[1:1 + 2 * pairs:2], tallies[2:2 + 2 * pairs:2]
    slack = jnp.minimum(donor - 1, most - receiver)
    moved = jax.random.randint(jax.random.fold_in(own_key, 1), (pairs,), 0, 1 << 20) % (slack + 1)
    tallies = tallies.at[1:1 + 2 * pairs:2].set(donor - moved).at[2:2 + 2 * pairs:2].set(receiver + moved)
    return tallies[jax.random.permutation(jax.random.fold_in(own_key, 2), amount)]


def bell_draw(rng, shape, width, limit, split=(), held_as=jnp.bfloat16):
    drawn = jax.random.normal(rng, shape, jnp.float32) * width
    if len(split) > 0:
        drawn = levels(rng, shape, split, -0.22, 0.18) * drawn
    return jnp.clip(drawn, min=-limit, max=limit).astype(held_as)


def setup_inputs(seed: int = 0, part: int = 0) -> dict:
    arg_keys = jax.random.split(jax.random.key(seed), 10)
    part_keys = jax.random.split(jax.random.fold_in(arg_keys[9], part), 10)
    return {
        "patches": bell_draw(part_keys[0], (SEQS, LEN, D), 1.0, 6.0, ((0, 4), (1, 4))),
        "segment_ids": jax.vmap(lambda own: jnp.searchsorted(jnp.cumsum(ragged_sizes(own, SEGS, LEN, SEG_MOST, 2)), jnp.arange(LEN), side="right"))(jax.random.split(part_keys[1], SEQS)).reshape((SEQS, LEN)).astype(jnp.int32),
        "patch_rows": touch_ends(jax.random.randint(part_keys[2], (SEQS, LEN), 0, GRID), jax.random.fold_in(part_keys[2], 1), 0, GRID - 1).astype(jnp.int32),
        "patch_cols": touch_ends(jax.random.randint(part_keys[3], (SEQS, LEN), 0, GRID), jax.random.fold_in(part_keys[3], 1), 0, GRID - 1).astype(jnp.int32),
        "row_table": bell_draw(arg_keys[4], (GRID, D), 0.5, 3.0),
        "col_table": bell_draw(arg_keys[5], (GRID, D), 0.5, 3.0),
        "norm_gain": jnp.clip(1.0 + 0.18 * jax.random.normal(arg_keys[6], (D,), jnp.float32), 0.1, 1.9),
        "qkv_weight": draw_qkv_weight(jax.random.fold_in(arg_keys[9], 71), part),
        "out_weight": bell_draw(arg_keys[8], (D, D), D ** -0.5, 0.1875, ((1, 4),)),
    }


floor_score = -1e+30
epsilon = 1e-06

def reference(patches, segment_ids, patch_rows, patch_cols, row_table, col_table, norm_gain, qkv_weight, out_weight):
    model_width = D
    head_count = HEADS
    head_size = model_width // head_count
    score_scale = 1.0 / head_size ** 0.5
    embedded = patches.astype(jnp.float32) + row_table[patch_rows].astype(jnp.float32) + col_table[patch_cols].astype(jnp.float32)
    average = lax.optimization_barrier(jnp.mean(embedded, axis=-1, keepdims=True))
    centered = embedded - average
    variance = lax.optimization_barrier(jnp.mean(centered * centered, axis=-1, keepdims=True))
    normed = (centered * lax.rsqrt(variance + epsilon) * norm_gain).astype(jnp.bfloat16)
    flat_normed = normed.reshape(-1, model_width)
    qkv = jnp.dot(flat_normed, qkv_weight, preferred_element_type=jnp.float32).astype(jnp.bfloat16)
    qkv = qkv.reshape(SEQS, LEN, 3 * model_width)

    def one_sequence(operands):
        packed, labels = operands
        queries = packed[:, :model_width].reshape(LEN, head_count, head_size).transpose(1, 0, 2)
        key_rows = packed[:, model_width:2 * model_width].reshape(LEN, head_count, head_size).transpose(1, 0, 2)
        value_rows = packed[:, 2 * model_width:].reshape(LEN, head_count, head_size).transpose(1, 0, 2)
        same_segment = labels[:, None] == labels[None, :]

        def one_head(head_operands):
            head_q, head_k, head_v = head_operands
            scores = jnp.dot(head_q, head_k.T, preferred_element_type=jnp.float32) * score_scale
            masked = jnp.where(same_segment, scores, floor_score)
            highest = lax.optimization_barrier(jnp.max(masked, axis=-1, keepdims=True))
            raised = jnp.where(same_segment, jnp.exp(masked - highest), 0.0)
            row_sums = lax.optimization_barrier(jnp.sum(raised, axis=-1, keepdims=True))
            mixed = jnp.dot(raised.astype(jnp.bfloat16), head_v, preferred_element_type=jnp.float32) / row_sums
            return mixed.astype(jnp.bfloat16)
        per_head = lax.map(one_head, (queries, key_rows, value_rows))
        return per_head.transpose(1, 0, 2).reshape(LEN, model_width)
    context = lax.map(one_sequence, (qkv, segment_ids))
    attended = jnp.dot(context.reshape(-1, model_width), out_weight, preferred_element_type=jnp.float32)
    encoded = embedded.reshape(-1, model_width) + attended
    return encoded.astype(jnp.bfloat16).reshape(SEQS, LEN, model_width)
```

```python
import functools

import jax
import jax.numpy as jnp
from jax import lax
from jax.experimental import pallas as pl
from jax.experimental.pallas import tpu as pltpu
from jax.sharding import PartitionSpec as P

HEADS = 16
floor_score = -1e30
epsilon = 1e-06
VM = pl.BlockSpec(memory_space=pltpu.VMEM)
SM = pl.BlockSpec(memory_space=pltpu.SMEM)
PAD = 16


def call(kernel, outs, args, specs, flops, scratch=(), name=None):
    moved = sum(a.size * a.dtype.itemsize for a in (*args, *outs))
    return pl.pallas_call(
        kernel,
        out_shape=outs,
        in_specs=specs,
        out_specs=[VM] * len(outs),
        scratch_shapes=scratch,
        name=name,
        cost_estimate=pl.CostEstimate(flops=flops, bytes_accessed=moved, transcendentals=0),
    )(*args)


def embed_kernel(patches, rows, cols, segs, row_table, col_table, gain, embedded, block):
    length, grid = patches.shape[0], row_table.shape[0]
    level = lax.broadcasted_iota(jnp.int32, (grid, length), 0)
    row_hot = jnp.where(rows[...] == level, 1.0, 0.0).T.astype(jnp.bfloat16)
    col_hot = jnp.where(cols[...] == level, 1.0, 0.0).T.astype(jnp.bfloat16)
    x = (
        patches[...].astype(jnp.float32)
        + jnp.dot(row_hot, row_table[...], preferred_element_type=jnp.float32)
        + jnp.dot(col_hot, col_table[...], preferred_element_type=jnp.float32)
    )
    embedded[...] = x
    centered = x - jnp.mean(x, axis=-1, keepdims=True)
    variance = jnp.mean(centered * centered, axis=-1, keepdims=True)
    block[:length, :] = (centered * lax.rsqrt(variance + epsilon) * gain[...]).astype(jnp.bfloat16)
    block[length:, :] = jnp.zeros((PAD, block.shape[1]), jnp.bfloat16)
    block[length:, :length] = jnp.broadcast_to(
        segs[...].astype(jnp.float32), (PAD, length)
    ).astype(jnp.bfloat16)


def qkv_kernel(slots, pieces, tile, scale, order, *refs):
    blocks, weights, (q_out, kv_out) = refs[:slots], refs[slots : slots + pieces], refs[slots + pieces :]
    length = blocks[0].shape[0] - PAD
    depth, width = weights[0].shape
    third = width // 3

    for slot in range(slots):
        rows = pl.ds(slot * length, length)
        for first in range(0, width, tile):
            total = None
            for piece in range(pieces):
                lanes = pl.ds(pl.multiple_of(order[piece] * depth, depth), depth)
                part = jnp.dot(
                    blocks[slot][:length, lanes],
                    weights[piece][:, first : first + tile],
                    preferred_element_type=jnp.float32,
                )
                total = part if total is None else total + part
            total = total.astype(jnp.bfloat16)
            if first < third:
                q_out[rows, first : first + tile] = total * jnp.bfloat16(scale)
            else:
                kv_out[rows, first - third : first - third + tile] = total
    kv_out[slots * length :, :] = jnp.zeros((PAD, 2 * third), jnp.bfloat16)
    for slot in range(slots):
        kv_out[pl.ds(slots * length + slot, 1), :length] = blocks[slot][length : length + 1, :length]


def attend_kernel(slots, slot, length, head, q, near, far, out, bias):
    half = slots * length
    third = q.shape[1]
    here = near[half:, :length].astype(jnp.float32)
    mine = here.T[:, slot : slot + 1]
    for side, keys in enumerate((near, far)):
        labels = keys[half:, :length].astype(jnp.float32)
        for j in range(slots):
            first = side * half + j * length
            bias[:, first : first + length] = jnp.where(
                mine == labels[j : j + 1, :], 0.0, floor_score
            )
    lane = lax.broadcasted_iota(jnp.int32, (length, 2 * head), 1)
    nt = (((1,), (1,)), ((), ()))

    def pair(index, carry):
        lanes = pl.ds(pl.multiple_of(index * 2 * head, 2 * head), 2 * head)
        values = pl.ds(pl.multiple_of(third + index * 2 * head, 2 * head), 2 * head)
        both = q[:, lanes]
        mixed = []
        for low in (True, False):
            mask = (lane < head) if low else (lane >= head)
            one = jnp.where(mask, both, jnp.zeros_like(both))
            scores = [
                lax.dot_general(one, keys[:half, lanes], nt, preferred_element_type=jnp.float32)
                + bias[:, side * half : (side + 1) * half]
                for side, keys in enumerate((near, far))
            ]
            highest = jnp.maximum(
                jnp.max(scores[0], axis=-1, keepdims=True), jnp.max(scores[1], axis=-1, keepdims=True)
            )
            raised = [jnp.exp(s - highest) for s in scores]
            total = jnp.sum(raised[0], axis=-1, keepdims=True) + jnp.sum(
                raised[1], axis=-1, keepdims=True
            )
            product = sum(
                jnp.dot(r.astype(jnp.bfloat16), keys[:half, values], preferred_element_type=jnp.float32)
                for r, keys in zip(raised, (near, far))
            )
            mixed.append(product / total)
        out[:, lanes] = jnp.where(lane < head, mixed[0], mixed[1]).astype(jnp.bfloat16)
        return carry

    lax.fori_loop(0, third // (2 * head), pair, 0)


def out_kernel(slots, pieces, places, order, embedded, *refs):
    contexts, weights, out, context = refs[:slots], refs[slots : slots + pieces], refs[-2], refs[-1]
    width = contexts[0].shape[1]
    for slot in range(slots):
        lanes = pl.ds(pl.multiple_of(places[slot] * width, width), width)
        context[:, lanes] = contexts[slot][...]
    span = weights[0].shape[1]
    for piece in range(pieces):
        lanes = pl.ds(pl.multiple_of(order[piece] * span, span), span)
        out[:, lanes] = (
            embedded[:, lanes]
            + jnp.dot(context[...], weights[piece][...], preferred_element_type=jnp.float32)
        ).astype(jnp.bfloat16)


def body(
    patches, segment_ids, patch_rows, patch_cols, row_table, col_table, norm_gain, qkv_weight, out_weight
):
    n, lanes = lax.axis_size("ctx"), lax.axis_size("fsdp")
    half, chips = n // 2, lanes // 2
    z, f = lax.axis_index("ctx"), lax.axis_index("fsdp")
    length, model = patches.shape[1:]
    head = model // HEADS
    group = model // half
    place = z % half

    def spread(j):
        pairs = []
        for a in range(n):
            for b in range(lanes):
                core = b % 2
                to_core = core if a // half == core else 1 - core
                to = core * half + (a % half + j) % half
                pairs.append((a * lanes + b, to * lanes + b - core + to_core))
        return pairs

    def along(value, by):
        return lax.ppermute(
            value, "fsdp", [(i, (i + 2 * by) % lanes) for i in range(lanes)]
        )

    def partner(value):
        return lax.ppermute(value, "fsdp", [(i, i ^ 1) for i in range(lanes)])

    def gather(piece):
        own = [piece] + [along(piece, by) for by in range(1, chips)]
        return own + [partner(p) for p in own]

    sources = [2 * ((f // 2 - by) % chips) + f % 2 for by in range(chips)]
    order = jnp.stack(sources + [s ^ 1 for s in sources]).astype(jnp.int32)
    depth = qkv_weight.shape[0]
    share = lax.dynamic_index_in_dim(
        qkv_weight.reshape(depth, 3, half, group), place, axis=2, keepdims=False
    ).reshape(depth, 3 * group)
    weights = gather(share)

    shape = jax.ShapeDtypeStruct
    embedded, block = call(
        embed_kernel,
        [shape((length, model), jnp.float32), shape((length + PAD, model), jnp.bfloat16)],
        (
            patches[0],
            patch_rows,
            patch_cols,
            segment_ids,
            row_table,
            col_table,
            norm_gain.reshape(1, model),
        ),
        [VM] * 7,
        4 * length * row_table.shape[0] * model,
        name="embed",
    )
    blocks = [lax.ppermute(block, ("ctx", "fsdp"), spread(j)) for j in range(half)]
    queries, kv = call(
        functools.partial(qkv_kernel, half, lanes, min(group, 256), 1.0 / head**0.5),
        [
            shape((half * length, group), jnp.bfloat16),
            shape((half * length + PAD, 2 * group), jnp.bfloat16),
        ],
        (order, *blocks, *weights),
        [SM] + [VM] * (half + lanes),
        2 * half * length * model * 3 * group,
        name="qkv",
    )
    other = partner(kv)
    out_weights = gather(out_weight)
    contexts = []
    for j in range(half):
        (context,) = call(
            functools.partial(attend_kernel, half, j, length, head),
            [shape((length, group), jnp.bfloat16)],
            (queries[j * length : (j + 1) * length], kv, other),
            [VM] * 3,
            8 * length * half * length * 2 * group,
            scratch=[pltpu.VMEM((length, 2 * half * length), jnp.float32)],
            name=f"attend{j}",
        )
        back = [(b, a) for a, b in spread(j)]
        contexts.append(lax.ppermute(context, ("ctx", "fsdp"), back))
    places = jnp.stack([(place + j) % half for j in range(half)]).astype(jnp.int32)
    (encoded,) = call(
        functools.partial(out_kernel, half, lanes),
        [shape((length, model), jnp.bfloat16)],
        (places, order, embedded, *contexts, *out_weights),
        [SM, SM] + [VM] * (1 + half + lanes),
        2 * length * model * model,
        scratch=[pltpu.VMEM((length, model), jnp.bfloat16)],
        name="out",
    )
    return encoded[None]


def solution(mesh):
    return jax.shard_map(
        body,
        mesh=mesh,
        in_specs=(
            P(("groups", "fsdp"), "ctx", None),
            P(("groups", "fsdp"), "ctx"),
            P(("groups", "fsdp"), "ctx"),
            P(("groups", "fsdp"), "ctx"),
            P(),
            P(),
            P(),
            P("fsdp", None),
            P(None, "fsdp"),
        ),
        out_specs=P(("groups", "fsdp"), "ctx", None),
        check_vma=False,
    )
```

```python
import functools

import jax
import jax.numpy as jnp
from jax import lax
from jax.experimental import pallas as pl
from jax.experimental.pallas import tpu as pltpu
from jax.sharding import PartitionSpec as P


HEADS = 16
floor_score = -1e30
epsilon = 1e-06
VM = pl.BlockSpec(memory_space=pltpu.VMEM)
SM = pl.BlockSpec(memory_space=pltpu.SMEM)
PAD = 16


def call(kernel, outs, args, specs, flops, scratch=()):
    moved = sum(a.size * a.dtype.itemsize for a in (*args, *outs))
    return pl.pallas_call(
        kernel,
        out_shape=outs,
        in_specs=specs,
        out_specs=[VM] * len(outs),
        scratch_shapes=scratch,
        cost_estimate=pl.CostEstimate(flops=flops, bytes_accessed=moved, transcendentals=0),
    )(*args)


def embed_kernel(patches, rows, cols, segs, row_table, col_table, gain, embedded, block):
    length, grid = patches.shape[0], row_table.shape[0]
    level = lax.broadcasted_iota(jnp.int32, (grid, length), 0)
    row_hot = jnp.where(rows[...] == level, 1.0, 0.0).T.astype(jnp.bfloat16)
    col_hot = jnp.where(cols[...] == level, 1.0, 0.0).T.astype(jnp.bfloat16)
    x = (
        patches[...].astype(jnp.float32)
        + jnp.dot(row_hot, row_table[...], preferred_element_type=jnp.float32)
        + jnp.dot(col_hot, col_table[...], preferred_element_type=jnp.float32)
    )
    embedded[...] = x
    centered = x - jnp.mean(x, axis=-1, keepdims=True)
    variance = jnp.mean(centered * centered, axis=-1, keepdims=True)
    block[:length, :] = (centered * lax.rsqrt(variance + epsilon) * gain[...]).astype(jnp.bfloat16)
    block[length:, :] = jnp.zeros((PAD, block.shape[1]), jnp.bfloat16)
    block[length:, :length] = jnp.broadcast_to(
        segs[...].astype(jnp.float32), (PAD, length)
    ).astype(jnp.bfloat16)


def qkv_kernel(slots, pieces, tile, scale, order, *refs):
    blocks, weights, outs = refs[:slots], refs[slots : slots + pieces], refs[slots + pieces :]
    q_outs, kv_out = outs[:-1], outs[-1]
    length = blocks[0].shape[0] - PAD
    depth, width = weights[0].shape
    third = width // 3

    for slot in range(slots):
        rows = pl.ds(slot * length, length)
        for first in range(0, width, tile):
            total = None
            for piece in range(pieces):
                lanes = pl.ds(pl.multiple_of(order[piece] * depth, depth), depth)
                part = jnp.dot(
                    blocks[slot][:length, lanes],
                    weights[piece][:, first : first + tile],
                    preferred_element_type=jnp.float32,
                )
                total = part if total is None else total + part
            total = total.astype(jnp.bfloat16)
            if first < third:
                q_outs[slot][:, first : first + tile] = total * jnp.bfloat16(scale)
            else:
                kv_out[rows, first - third : first - third + tile] = total
    kv_out[slots * length :, :] = jnp.zeros((PAD, 2 * third), jnp.bfloat16)
    for slot in range(slots):
        kv_out[pl.ds(slots * length + slot, 1), :length] = blocks[slot][length : length + 1, :length]


def attend_kernel(slots, slot, length, head, q, near, far, out, hot, gate):
    half = slots * length
    third = q.shape[1]
    level = lax.broadcasted_iota(jnp.int32, (128, length), 0).astype(jnp.float32)
    for side, keys in enumerate((near, far)):
        labels = keys[half:, :length].astype(jnp.float32)
        for j in range(slots):
            match = labels[j : j + 1, :] == level
            gate[pl.ds(side * half + j * length, length), :] = (
                jnp.where(match, 0.0, floor_score).T.astype(jnp.bfloat16)
            )
            if side == 0 and j == slot:
                hot[...] = jnp.where(match, 1.0, 0.0).T.astype(jnp.bfloat16)
    lane = lax.broadcasted_iota(jnp.int32, (length, 2 * head), 1)
    nt = (((1,), (1,)), ((), ()))
    ones = jnp.ones((half, 2 * head), jnp.bfloat16)

    def pair(index, carry):
        lanes = pl.ds(pl.multiple_of(index * 2 * head, 2 * head), 2 * head)
        values = pl.ds(pl.multiple_of(third + index * 2 * head, 2 * head), 2 * head)
        both = q[:, lanes]
        mixed = []
        for low in (True, False):
            mask = (lane < head) if low else (lane >= head)
            one = jnp.concatenate([jnp.where(mask, both, jnp.zeros_like(both)), hot[...]], axis=1)
            scores = [
                lax.dot_general(
                    one,
                    jnp.concatenate([keys[:half, lanes], gate[pl.ds(side * half, half), :]], axis=1),
                    nt,
                    preferred_element_type=jnp.float32,
                )
                for side, keys in enumerate((near, far))
            ]
            highest = jnp.maximum(
                jnp.max(scores[0], axis=-1, keepdims=True), jnp.max(scores[1], axis=-1, keepdims=True)
            )
            product = sum(
                jnp.dot(
                    jnp.exp(s - highest).astype(jnp.bfloat16),
                    jnp.concatenate([keys[:half, values], ones], axis=1),
                    preferred_element_type=jnp.float32,
                )
                for s, keys in zip(scores, (near, far))
            )
            mixed.append(product[:, : 2 * head] / product[:, 2 * head :])
        out[:, lanes] = jnp.where(lane < head, mixed[0], mixed[1]).astype(jnp.bfloat16)
        return carry

    lax.fori_loop(0, third // (2 * head), pair, 0)


def out_kernel(slots, pieces, places, order, embedded, *refs):
    contexts, weights, out, context = refs[:slots], refs[slots : slots + pieces], refs[-2], refs[-1]
    width = contexts[0].shape[1]
    for slot in range(slots):
        lanes = pl.ds(pl.multiple_of(places[slot] * width, width), width)
        context[:, lanes] = contexts[slot][...]
    span = weights[0].shape[1]
    for piece in range(pieces):
        lanes = pl.ds(pl.multiple_of(order[piece] * span, span), span)
        out[:, lanes] = (
            embedded[:, lanes]
            + jnp.dot(context[...], weights[piece][...], preferred_element_type=jnp.float32)
        ).astype(jnp.bfloat16)


def body(
    patches, segment_ids, patch_rows, patch_cols, row_table, col_table, norm_gain, qkv_weight, out_weight
):
    n, lanes = lax.axis_size("ctx"), lax.axis_size("fsdp")
    half, chips = n // 2, lanes // 2
    z, f = lax.axis_index("ctx"), lax.axis_index("fsdp")
    length, model = patches.shape[1:]
    head = model // HEADS
    group = model // half
    place = z % half

    def spread(j):
        pairs = []
        for a in range(n):
            for b in range(lanes):
                core = b % 2
                to_core = core if a // half == core else 1 - core
                to = core * half + (a % half + j) % half
                pairs.append((a * lanes + b, to * lanes + b - core + to_core))
        return pairs

    def along(value, by):
        return lax.ppermute(value, "fsdp", [(i, (i + 2 * by) % lanes) for i in range(lanes)])

    def partner(value):
        return lax.ppermute(value, "fsdp", [(i, i ^ 1) for i in range(lanes)])

    def gather(piece):
        own = [piece] + [along(piece, by) for by in range(1, chips)]
        return own + [partner(p) for p in own]

    sources = [2 * ((f // 2 - by) % chips) + f % 2 for by in range(chips)]
    order = jnp.stack(sources + [s ^ 1 for s in sources]).astype(jnp.int32)
    depth = qkv_weight.shape[0]
    share = jnp.concatenate(
        [
            lax.dynamic_slice(qkv_weight, (0, part * model + place * group), (depth, group))
            for part in range(3)
        ],
        axis=1,
    )
    weights = gather(share)

    shape = jax.ShapeDtypeStruct
    embedded, block = call(
        embed_kernel,
        [shape((length, model), jnp.float32), shape((length + PAD, model), jnp.bfloat16)],
        (
            patches[0],
            patch_rows,
            patch_cols,
            segment_ids,
            row_table,
            col_table,
            norm_gain.reshape(1, model),
        ),
        [VM] * 7,
        4 * length * row_table.shape[0] * model,
    )
    blocks = []
    for j in range(half):
        blocks.append(lax.ppermute(block, ("ctx", "fsdp"), spread(j)))
    *queries, kv = call(
        functools.partial(qkv_kernel, half, lanes, min(group, 256), 1.0 / head**0.5),
        [
            *[shape((length, group), jnp.bfloat16)] * half,
            shape((half * length + PAD, 2 * group), jnp.bfloat16),
        ],
        (order, *blocks, *weights),
        [SM] + [VM] * (half + lanes),
        2 * half * length * model * 3 * group,
    )
    other = partner(kv)
    out_weights = gather(out_weight)
    contexts = []
    for j in range(half):
        (context,) = call(
            functools.partial(attend_kernel, half, j, length, head),
            [shape((length, group), jnp.bfloat16)],
            (queries[j], kv, other),
            [VM] * 3,
            8 * length * half * length * 2 * group,
            scratch=[
                pltpu.VMEM((length, 128), jnp.bfloat16),
                pltpu.VMEM((2 * half * length, 128), jnp.bfloat16),
            ],
        )
        back = [(b, a) for a, b in spread(j)]
        contexts.append(lax.ppermute(context, ("ctx", "fsdp"), back))
    places = jnp.stack([(place + j) % half for j in range(half)]).astype(jnp.int32)
    (encoded,) = call(
        functools.partial(out_kernel, half, lanes),
        [shape((length, model), jnp.bfloat16)],
        (places, order, embedded, *contexts, *out_weights),
        [SM, SM] + [VM] * (1 + half + lanes),
        2 * length * model * model,
        scratch=[pltpu.VMEM((length, model), jnp.bfloat16)],
    )
    return encoded[None]


def solution(mesh):
    return jax.shard_map(
        body,
        mesh=mesh,
        in_specs=(
            P(("groups", "fsdp"), "ctx", None),
            P(("groups", "fsdp"), "ctx"),
            P(("groups", "fsdp"), "ctx"),
            P(("groups", "fsdp"), "ctx"),
            P(),
            P(),
            P(),
            P("fsdp", None),
            P(None, "fsdp"),
        ),
        out_specs=P(("groups", "fsdp"), "ctx", None),
        check_vma=False,
    )
```

```python
import functools

import jax
import jax.numpy as jnp
from jax import lax
from jax.experimental import pallas as pl
from jax.experimental.pallas import tpu as pltpu
from jax.sharding import PartitionSpec as P


HEADS = 16
floor_score = -1e30
epsilon = 1e-06
VM = pl.BlockSpec(memory_space=pltpu.VMEM)
SM = pl.BlockSpec(memory_space=pltpu.SMEM)
PAD = 16


HB = pl.BlockSpec(memory_space=pltpu.HBM)


def call(kernel, outs, args, specs, flops, scratch=(), limit=16 << 20):
    moved = sum(a.size * a.dtype.itemsize for a in (*args, *outs))
    return pl.pallas_call(
        kernel,
        out_shape=outs,
        in_specs=specs,
        out_specs=[VM] * len(outs),
        scratch_shapes=scratch,
        compiler_params=pltpu.CompilerParams(vmem_limit_bytes=limit),
        cost_estimate=pl.CostEstimate(flops=flops, bytes_accessed=moved, transcendentals=0),
    )(*args)


def embed_kernel(place, *refs):
    inputs, weight, (embedded, block, share) = refs[:7], refs[7], refs[8:11]
    local, sems = refs[11:18], refs[18]
    copies = [pltpu.make_async_copy(a, b, sems.at[i]) for i, (a, b) in enumerate(zip(inputs, local))]
    group = share.shape[1] // 3
    for part in range(3):
        first = pl.multiple_of(part * (weight.shape[1] // 3) + place[0] * group, group)
        copies.append(
            pltpu.make_async_copy(
                weight.at[:, pl.ds(first, group)],
                share.at[:, pl.ds(part * group, group)],
                sems.at[7 + part],
            )
        )
    for copy in copies:
        copy.start()
    for copy in copies[:7]:
        copy.wait()
    patches, rows, cols, segs, row_table, col_table, gain = local
    length, grid = patches.shape[0], row_table.shape[0]
    level = lax.broadcasted_iota(jnp.int32, (grid, length), 0)
    row_hot = jnp.where(rows[...] == level, 1.0, 0.0).T.astype(jnp.bfloat16)
    col_hot = jnp.where(cols[...] == level, 1.0, 0.0).T.astype(jnp.bfloat16)
    x = (
        patches[...].astype(jnp.float32)
        + jnp.dot(row_hot, row_table[...], preferred_element_type=jnp.float32)
        + jnp.dot(col_hot, col_table[...], preferred_element_type=jnp.float32)
    )
    embedded[...] = x
    centered = x - jnp.mean(x, axis=-1, keepdims=True)
    variance = jnp.mean(centered * centered, axis=-1, keepdims=True)
    block[:length, :] = (centered * lax.rsqrt(variance + epsilon) * gain[...]).astype(jnp.bfloat16)
    block[length:, :] = jnp.zeros((PAD, block.shape[1]), jnp.bfloat16)
    block[length:, :length] = jnp.broadcast_to(
        segs[...].astype(jnp.float32), (PAD, length)
    ).astype(jnp.bfloat16)
    for copy in copies[7:]:
        copy.wait()


def qkv_kernel(pieces, parts, tile, scale, order, *refs):
    blocks, weights = refs[:parts], refs[parts : parts + pieces]
    q_out, kv_out = refs[parts + pieces : parts + pieces + 2]
    length = q_out.shape[0]
    depth, width = weights[0].shape
    third = width // 3
    block = blocks[0]
    if parts > 1:
        block = refs[-1]
        block[...] = sum(b[...] for b in blocks[1:]) + blocks[0][...]
    for first in range(0, width, tile):
        total = None
        for piece in range(pieces):
            lanes = pl.ds(pl.multiple_of(order[piece] * depth, depth), depth)
            part = jnp.dot(
                block[:length, lanes],
                weights[piece][:, first : first + tile],
                preferred_element_type=jnp.float32,
            )
            total = part if total is None else total + part
        total = total.astype(jnp.bfloat16)
        if first < third:
            q_out[:, first : first + tile] = total * jnp.bfloat16(scale)
        else:
            kv_out[:length, first - third : first - third + tile] = total
    kv_out[length:, :] = jnp.zeros((PAD, 2 * third), jnp.bfloat16)
    kv_out[length:, :length] = block[length:, :length]


def attend_kernel(slots, slot, head, q, *refs):
    keys, (out, hot, gate) = refs[: 2 * slots], refs[2 * slots :]
    length, third = q.shape
    level = lax.broadcasted_iota(jnp.int32, (128, length), 0).astype(jnp.float32)
    for j, ref in enumerate(keys):
        match = ref[length : length + 1, :length].astype(jnp.float32) == level
        gate[pl.ds(j * length, length), :] = (
            jnp.where(match, 0.0, floor_score).T.astype(jnp.bfloat16)
        )
        if j == slot:
            hot[...] = jnp.where(match, 1.0, 0.0).T.astype(jnp.bfloat16)
    lane = lax.broadcasted_iota(jnp.int32, (length, 2 * head), 1)
    nt = (((1,), (1,)), ((), ()))
    ones = jnp.ones((length, 2 * head), jnp.bfloat16)

    def pair(index, carry):
        lanes = pl.ds(pl.multiple_of(index * 2 * head, 2 * head), 2 * head)
        values = pl.ds(pl.multiple_of(third + index * 2 * head, 2 * head), 2 * head)
        both = q[:, lanes]
        mixed = []
        for low in (True, False):
            mask = (lane < head) if low else (lane >= head)
            one = jnp.concatenate([jnp.where(mask, both, jnp.zeros_like(both)), hot[...]], axis=1)
            scores = [
                lax.dot_general(
                    one,
                    jnp.concatenate([ref[:length, lanes], gate[pl.ds(j * length, length), :]], axis=1),
                    nt,
                    preferred_element_type=jnp.float32,
                )
                for j, ref in enumerate(keys)
            ]
            highest = functools.reduce(
                jnp.maximum, [jnp.max(s, axis=-1, keepdims=True) for s in scores]
            )
            product = sum(
                jnp.dot(
                    jnp.exp(s - highest).astype(jnp.bfloat16),
                    jnp.concatenate([ref[:length, values], ones], axis=1),
                    preferred_element_type=jnp.float32,
                )
                for s, ref in zip(scores, keys)
            )
            mixed.append(product[:, : 2 * head] / product[:, 2 * head :])
        out[:, lanes] = jnp.where(lane < head, mixed[0], mixed[1]).astype(jnp.bfloat16)
        return carry

    lax.fori_loop(0, third // (2 * head), pair, 0)


def out_kernel(slots, pieces, places, order, embedded, *refs):
    contexts, weights, out, context = refs[:slots], refs[slots : slots + pieces], refs[-2], refs[-1]
    width = contexts[0].shape[1]
    for slot in range(slots):
        lanes = pl.ds(pl.multiple_of(places[slot] * width, width), width)
        context[:, lanes] = contexts[slot][...]
    span = weights[0].shape[1]
    for piece in range(pieces):
        lanes = pl.ds(pl.multiple_of(order[piece] * span, span), span)
        out[:, lanes] = (
            embedded[:, lanes]
            + jnp.dot(context[...], weights[piece][...], preferred_element_type=jnp.float32)
        ).astype(jnp.bfloat16)


def body(
    patches, segment_ids, patch_rows, patch_cols, row_table, col_table, norm_gain, qkv_weight, out_weight
):
    n, lanes = lax.axis_size("ctx"), lax.axis_size("fsdp")
    half, chips = n // 2, lanes // 2
    z, f = lax.axis_index("ctx"), lax.axis_index("fsdp")
    length, model = patches.shape[1:]
    head = model // HEADS
    group = model // half
    place = z % half

    def spread(j, near=True, far=True):
        pairs = []
        for a in range(n):
            for b in range(lanes):
                core = b % 2
                here = a // half == core
                to = core * half + (a % half + j) % half
                if near if here else far:
                    pairs.append((a * lanes + b, to * lanes + b - core + (core if here else 1 - core)))
        return pairs

    def around(j):
        return [
            (a * lanes + b, (a - a % half + (a % half + j) % half) * lanes + b)
            for a in range(n)
            for b in range(lanes)
            if a // half != b % 2
        ]

    def send(value, pairs):
        return lax.ppermute(value, ("ctx", "fsdp"), pairs)

    def along(value, by):
        return lax.ppermute(value, "fsdp", [(i, (i + 2 * by) % lanes) for i in range(lanes)])

    def partner(value):
        return lax.ppermute(value, "fsdp", [(i, i ^ 1) for i in range(lanes)])

    def gather(piece):
        own = [piece] + [along(piece, by) for by in range(1, chips)]
        return own + [partner(p) for p in own]

    sources = [2 * ((f // 2 - by) % chips) + f % 2 for by in range(chips)]
    order = jnp.stack(sources + [s ^ 1 for s in sources]).astype(jnp.int32)
    depth = qkv_weight.shape[0]
    shape = jax.ShapeDtypeStruct
    inputs = (
        patches[0],
        patch_rows,
        patch_cols,
        segment_ids,
        row_table,
        col_table,
        norm_gain.reshape(1, model),
    )
    embedded, block, share = call(
        embed_kernel,
        [
            shape((length, model), jnp.float32),
            shape((length + PAD, model), jnp.bfloat16),
            shape((depth, 3 * group), jnp.bfloat16),
        ],
        (
            place.reshape(1).astype(jnp.int32),
            *[pltpu.with_memory_space_constraint(a, pltpu.HBM) for a in (*inputs, qkv_weight)],
        ),
        [SM] + [HB] * 8,
        4 * length * row_table.shape[0] * model,
        scratch=[pltpu.VMEM(a.shape, a.dtype) for a in inputs] + [pltpu.SemaphoreType.DMA((10,))],
    )
    weights = gather(share)
    out_weights = gather(out_weight)
    first = send(block, spread(0))
    blocks = [[first]] + [
        [send(block, spread(j, far=False)), send(first, around(j))]
        for j in range(1, half)
    ]
    queries, keys = [], []
    for parts in blocks:
        q, kv = call(
            functools.partial(qkv_kernel, lanes, len(parts), min(group, 256), 1.0 / head**0.5),
            [shape((length, group), jnp.bfloat16), shape((length + PAD, 2 * group), jnp.bfloat16)],
            (order, *parts, *weights),
            [SM] + [VM] * (len(parts) + lanes),
            2 * length * model * 3 * group,
            scratch=[pltpu.VMEM(block.shape, jnp.bfloat16)] * (len(parts) > 1),
        )
        queries.append(q)
        keys.append(kv)
    keys += [partner(kv) for kv in keys]
    contexts = []
    for j in range(half):
        (context,) = call(
            functools.partial(attend_kernel, half, j, head),
            [shape((length, group), jnp.bfloat16)],
            (queries[j], *keys),
            [VM] * (1 + 2 * half),
            8 * length * half * length * 2 * group,
            scratch=[
                pltpu.VMEM((length, 128), jnp.bfloat16),
                pltpu.VMEM((2 * half * length, 128), jnp.bfloat16),
            ],
        )
        contexts.append(send(context, [(b, a) for a, b in spread(j)]))
    places = jnp.stack([(place + j) % half for j in range(half)]).astype(jnp.int32)
    (encoded,) = call(
        functools.partial(out_kernel, half, lanes),
        [shape((length, model), jnp.bfloat16)],
        (places, order, embedded, *contexts, *out_weights),
        [SM, SM] + [VM] * (1 + half + lanes),
        2 * length * model * model,
        scratch=[pltpu.VMEM((length, model), jnp.bfloat16)],
    )
    return encoded[None]


def solution(mesh):
    return jax.shard_map(
        body,
        mesh=mesh,
        in_specs=(
            P(("groups", "fsdp"), "ctx", None),
            P(("groups", "fsdp"), "ctx"),
            P(("groups", "fsdp"), "ctx"),
            P(("groups", "fsdp"), "ctx"),
            P(),
            P(),
            P(),
            P("fsdp", None),
            P(None, "fsdp"),
        ),
        out_specs=P(("groups", "fsdp"), "ctx", None),
        check_vma=False,
    )
```

```python
import functools

import jax
import jax.numpy as jnp
from jax import lax
from jax.experimental import pallas as pl
from jax.experimental.pallas import tpu as pltpu
from jax.sharding import PartitionSpec as P


HEADS = 16
floor_score = -1e30
epsilon = 1e-06
VM = pl.BlockSpec(memory_space=pltpu.VMEM)
SM = pl.BlockSpec(memory_space=pltpu.SMEM)
PAD = 16
CUTS = 2


HB = pl.BlockSpec(memory_space=pltpu.HBM)


def call(kernel, outs, args, specs, flops, scratch=(), limit=16 << 20):
    moved = sum(a.size * a.dtype.itemsize for a in (*args, *outs))
    return pl.pallas_call(
        kernel,
        out_shape=outs,
        in_specs=specs,
        out_specs=[VM] * len(outs),
        scratch_shapes=scratch,
        compiler_params=pltpu.CompilerParams(vmem_limit_bytes=limit),
        cost_estimate=pl.CostEstimate(flops=flops, bytes_accessed=moved, transcendentals=0),
    )(*args)


def embedding(patches, rows, cols, row_table, col_table):
    length, grid = patches.shape[0], row_table.shape[0]
    level = lax.broadcasted_iota(jnp.int32, (grid, length), 0)
    row_hot = jnp.where(rows[...] == level, 1.0, 0.0).T.astype(jnp.bfloat16)
    col_hot = jnp.where(cols[...] == level, 1.0, 0.0).T.astype(jnp.bfloat16)
    return (
        patches[...].astype(jnp.float32)
        + jnp.dot(row_hot, row_table[...], preferred_element_type=jnp.float32)
        + jnp.dot(col_hot, col_table[...], preferred_element_type=jnp.float32)
    )


def embed_kernel(place, *refs):
    inputs, weight, share, blocks = refs[:7], refs[7], refs[8], refs[9 : 9 + CUTS]
    local, sems = refs[9 + CUTS : 16 + CUTS], refs[16 + CUTS]
    copies = [pltpu.make_async_copy(a, b, sems.at[i]) for i, (a, b) in enumerate(zip(inputs, local))]
    group = share.shape[1] // 3
    for part in range(3):
        first = pl.multiple_of(part * (weight.shape[1] // 3) + place[0] * group, group)
        copies.append(
            pltpu.make_async_copy(
                weight.at[:, pl.ds(first, group)],
                share.at[:, pl.ds(part * group, group)],
                sems.at[7 + part],
            )
        )
    for copy in copies:
        copy.start()
    for copy in copies[:7]:
        copy.wait()
    patches, rows, cols, row_table, col_table, segs, gain = local
    length = patches.shape[0]
    x = embedding(patches, rows, cols, row_table, col_table)
    centered = x - jnp.mean(x, axis=-1, keepdims=True)
    variance = jnp.mean(centered * centered, axis=-1, keepdims=True)
    normed = (centered * lax.rsqrt(variance + epsilon) * gain[...]).astype(jnp.bfloat16)
    labels = jnp.broadcast_to(segs[...].astype(jnp.float32), (PAD, length)).astype(jnp.bfloat16)
    cut = length // CUTS
    for i, block in enumerate(blocks):
        block[:cut, :] = normed[i * cut : (i + 1) * cut]
        block[cut:, :] = jnp.zeros((PAD, block.shape[1]), jnp.bfloat16)
        block[cut:, :cut] = labels[:, i * cut : (i + 1) * cut]
    for copy in copies[7:]:
        copy.wait()


def qkv_kernel(pieces, choose, tile, scale, order, own, *refs):
    ways, weights = (refs[:CUTS], refs[CUTS : 2 * CUTS]), refs[2 * CUTS : 2 * CUTS + pieces]
    q_out, kv_out, block = refs[2 * CUTS + pieces :]
    length = q_out.shape[0]
    depth, width = weights[0].shape
    third = width // 3
    cut = length // CUTS
    kv_out[length:, :] = jnp.zeros((PAD, 2 * third), jnp.bfloat16)
    for i, (one, two) in enumerate(zip(*ways)):
        if choose:
            part = jnp.where(own[0] == 1, one[...], two[...])
        else:
            part = one[...] + two[...]
        block[i * cut : (i + 1) * cut, :] = part[:cut]
        kv_out[length:, i * cut : (i + 1) * cut] = part[cut:, :cut]
    for first in range(0, width, tile):
        total = None
        for piece in range(pieces):
            lanes = pl.ds(pl.multiple_of(order[piece] * depth, depth), depth)
            part = jnp.dot(
                block[:, lanes],
                weights[piece][:, first : first + tile],
                preferred_element_type=jnp.float32,
            )
            total = part if total is None else total + part
        total = total.astype(jnp.bfloat16)
        if first < third:
            q_out[:, first : first + tile] = total * jnp.bfloat16(scale)
        else:
            kv_out[:length, first - third : first - third + tile] = total


def attend_kernel(slots, slot, head, q, *refs):
    keys, (out, hot, gate) = refs[: 2 * slots], refs[2 * slots :]
    length, third = q.shape
    level = lax.broadcasted_iota(jnp.int32, (128, length), 0).astype(jnp.float32)
    for j, ref in enumerate(keys):
        match = ref[length : length + 1, :length].astype(jnp.float32) == level
        gate[pl.ds(j * length, length), :] = (
            jnp.where(match, 0.0, floor_score).T.astype(jnp.bfloat16)
        )
        if j == slot:
            hot[...] = jnp.where(match, 1.0, 0.0).T.astype(jnp.bfloat16)
    lane = lax.broadcasted_iota(jnp.int32, (length, 2 * head), 1)
    nt = (((1,), (1,)), ((), ()))
    ones = jnp.ones((length, 2 * head), jnp.bfloat16)

    def pair(index, carry):
        lanes = pl.ds(pl.multiple_of(index * 2 * head, 2 * head), 2 * head)
        values = pl.ds(pl.multiple_of(third + index * 2 * head, 2 * head), 2 * head)
        both = q[:, lanes]
        mixed = []
        for low in (True, False):
            mask = (lane < head) if low else (lane >= head)
            one = jnp.concatenate([jnp.where(mask, both, jnp.zeros_like(both)), hot[...]], axis=1)
            scores = [
                lax.dot_general(
                    one,
                    jnp.concatenate([ref[:length, lanes], gate[pl.ds(j * length, length), :]], axis=1),
                    nt,
                    preferred_element_type=jnp.float32,
                )
                for j, ref in enumerate(keys)
            ]
            highest = functools.reduce(
                jnp.maximum, [jnp.max(s, axis=-1, keepdims=True) for s in scores]
            )
            product = sum(
                jnp.dot(
                    jnp.exp(s - highest).astype(jnp.bfloat16),
                    jnp.concatenate([ref[:length, values], ones], axis=1),
                    preferred_element_type=jnp.float32,
                )
                for s, ref in zip(scores, keys)
            )
            mixed.append(product[:, : 2 * head] / product[:, 2 * head :])
        out[:, lanes] = jnp.where(lane < head, mixed[0], mixed[1]).astype(jnp.bfloat16)
        return carry

    lax.fori_loop(0, third // (2 * head), pair, 0)


def first_kernel(slots, pieces, places, order, *refs):
    inputs, refs = refs[:5], refs[5:]
    contexts, weights = refs[: slots - 1], refs[slots - 1 : slots - 1 + pieces]
    out, kept = refs[slots - 1 + pieces : slots + 1 + pieces]
    local, sems = refs[slots + 1 + pieces : -1], refs[-1]
    copies = [pltpu.make_async_copy(a, b, sems.at[i]) for i, (a, b) in enumerate(zip(inputs, local))]
    for copy in copies:
        copy.start()
    for copy in copies:
        copy.wait()
    out[...] = embedding(*local)
    width, span = kept.shape[0], weights[0].shape[1]
    rows = [pl.ds(pl.multiple_of(places[j] * width, width), width) for j in range(slots)]
    for piece, weight in enumerate(weights):
        lanes = pl.ds(pl.multiple_of(order[piece] * span, span), span)
        kept[:, lanes] = weight[rows[-1], :]
        for context, row in zip(contexts, rows):
            out[:, lanes] += jnp.dot(context[...], weight[row, :], preferred_element_type=jnp.float32)


def last_kernel(base, context, weight, out):
    out[...] = (
        base[...] + jnp.dot(context[...], weight[...], preferred_element_type=jnp.float32)
    ).astype(out.dtype)


def body(
    patches, segment_ids, patch_rows, patch_cols, row_table, col_table, norm_gain, qkv_weight, out_weight
):
    n, lanes = lax.axis_size("ctx"), lax.axis_size("fsdp")
    half, chips = n // 2, lanes // 2
    z, f = lax.axis_index("ctx"), lax.axis_index("fsdp")
    length, model = patches.shape[1:]
    head = model // HEADS
    group = model // half
    place = z % half

    def spread(j, near=True, far=True):
        pairs = []
        for a in range(n):
            for b in range(lanes):
                core = b % 2
                here = a // half == core
                to = core * half + (a % half + j) % half
                if near if here else far:
                    pairs.append((a * lanes + b, to * lanes + b - core + (core if here else 1 - core)))
        return pairs

    def around(j):
        return [
            (a * lanes + b, (a - a % half + (a % half + j) % half) * lanes + b)
            for a in range(n)
            for b in range(lanes)
            if a // half != b % 2
        ]

    def send_cuts(values, pairs):
        return [send(value, pairs) for value in values]

    def send(value, pairs):
        return lax.ppermute(value, ("ctx", "fsdp"), pairs)

    def along(value, by):
        return lax.ppermute(value, "fsdp", [(i, (i + 2 * by) % lanes) for i in range(lanes)])

    def partner(value):
        return lax.ppermute(value, "fsdp", [(i, i ^ 1) for i in range(lanes)])

    def gather(piece):
        own = [piece] + [along(piece, by) for by in range(1, chips)]
        return own + [partner(p) for p in own]

    sources = [2 * ((f // 2 - by) % chips) + f % 2 for by in range(chips)]
    order = jnp.stack(sources + [s ^ 1 for s in sources]).astype(jnp.int32)
    depth = qkv_weight.shape[0]
    shape = jax.ShapeDtypeStruct
    inputs = (
        patches[0],
        patch_rows,
        patch_cols,
        row_table,
        col_table,
        segment_ids,
        norm_gain.reshape(1, model),
    )
    kept = [pltpu.with_memory_space_constraint(a, pltpu.HBM) for a in (*inputs, qkv_weight)]
    local = [pltpu.VMEM(a.shape, a.dtype) for a in inputs]
    share, *block = call(
        embed_kernel,
        [
            shape((depth, 3 * group), jnp.bfloat16),
            *[shape((length // CUTS + PAD, model), jnp.bfloat16)] * CUTS,
        ],
        (place.reshape(1).astype(jnp.int32), *kept),
        [SM] + [HB] * 8,
        4 * length * row_table.shape[0] * model,
        scratch=local + [pltpu.SemaphoreType.DMA((10,))],
    )
    weights = gather(share)
    out_weights = gather(out_weight)
    own = (z // half == f % 2).astype(jnp.int32).reshape(1)
    first = send_cuts(block, spread(0, near=False))
    blocks = [[block, first]] + [
        [send_cuts(block, spread(j, far=False)), send_cuts(first, around(j))]
        for j in range(1, half)
    ]
    queries, keys = [], []
    for j, parts in enumerate(blocks):
        q, kv = call(
            functools.partial(qkv_kernel, lanes, j == 0, min(group, 256), 1.0 / head**0.5),
            [shape((length, group), jnp.bfloat16), shape((length + PAD, 2 * group), jnp.bfloat16)],
            (order, own, *parts[0], *parts[1], *weights),
            [SM, SM] + [VM] * (2 * CUTS + lanes),
            2 * length * model * 3 * group,
            scratch=[pltpu.VMEM((length, model), jnp.bfloat16)],
        )
        queries.append(q)
        keys.append(kv)
    keys += [partner(kv) for kv in keys]
    contexts = []
    for j in range(half):
        (context,) = call(
            functools.partial(attend_kernel, half, j, head),
            [shape((length, group), jnp.bfloat16)],
            (queries[j], *keys),
            [VM] * (1 + 2 * half),
            8 * length * half * length * 2 * group,
            scratch=[
                pltpu.VMEM((length, 128), jnp.bfloat16),
                pltpu.VMEM((2 * half * length, 128), jnp.bfloat16),
            ],
        )
        contexts.append(send(context, [(b, a) for a, b in spread(j)]))
    places = jnp.stack([(place + j) % half for j in range(half)]).astype(jnp.int32)
    base, kept_rows = call(
        functools.partial(first_kernel, half, lanes),
        [shape((length, model), jnp.float32), shape((group, model), jnp.bfloat16)],
        (places, order, *kept[:5], *contexts[:-1], *out_weights),
        [SM, SM] + [HB] * 5 + [VM] * (half - 1 + lanes),
        2 * length * model * (model - group),
        scratch=local[:5] + [pltpu.SemaphoreType.DMA((5,))],
    )
    (encoded,) = call(
        last_kernel,
        [shape((length, model), jnp.bfloat16)],
        (base, contexts[-1], kept_rows),
        [VM] * 3,
        2 * length * model * group,
    )
    return encoded[None]


def solution(mesh):
    return jax.shard_map(
        body,
        mesh=mesh,
        in_specs=(
            P(("groups", "fsdp"), "ctx", None),
            P(("groups", "fsdp"), "ctx"),
            P(("groups", "fsdp"), "ctx"),
            P(("groups", "fsdp"), "ctx"),
            P(),
            P(),
            P(),
            P("fsdp", None),
            P(None, "fsdp"),
        ),
        out_specs=P(("groups", "fsdp"), "ctx", None),
        check_vma=False,
    )
```

```python
import functools

import jax
import jax.numpy as jnp
from jax import lax
from jax.experimental import pallas as pl
from jax.experimental.pallas import tpu as pltpu
from jax.sharding import PartitionSpec as P


HEADS = 16
floor_score = -1e30
epsilon = 1e-06
VM = pl.BlockSpec(memory_space=pltpu.VMEM)
PAD = 16
CUTS = 2


HB = pl.BlockSpec(memory_space=pltpu.HBM)


def here():
    half, lanes = lax.axis_size("ctx") // 2, lax.axis_size("fsdp")
    z, f = lax.axis_index("ctx"), lax.axis_index("fsdp")
    chips, core = lanes // 2, lax.rem(f, 2)
    sources = [2 * lax.rem(lax.div(f, 2) + chips - by, chips) + core for by in range(chips)]
    order = sources + [s + 1 - 2 * core for s in sources]
    return lax.rem(z, half), lax.div(z, half) == core, order


def call(kernel, outs, args, specs, flops, scratch=(), away=0):
    moved = sum(a.size * a.dtype.itemsize for a in (*args, *outs))
    return pl.pallas_call(
        kernel,
        out_shape=outs,
        in_specs=specs,
        out_specs=[VM] * (len(outs) - away) + [HB] * away,
        scratch_shapes=scratch,
        compiler_params=pltpu.CompilerParams(vmem_limit_bytes=16 << 20),
        cost_estimate=pl.CostEstimate(flops=flops, bytes_accessed=moved, transcendentals=0),
    )(*args)


def embedding(patches, rows, cols, row_table, col_table):
    length, grid = patches.shape[0], row_table.shape[0]
    level = lax.broadcasted_iota(jnp.int32, (grid, length), 0)
    row_hot = jnp.where(rows[...] == level, 1.0, 0.0).T.astype(jnp.bfloat16)
    col_hot = jnp.where(cols[...] == level, 1.0, 0.0).T.astype(jnp.bfloat16)
    return (
        patches[...].astype(jnp.float32)
        + jnp.dot(row_hot, row_table[...], preferred_element_type=jnp.float32)
        + jnp.dot(col_hot, col_table[...], preferred_element_type=jnp.float32)
    )


def embed_kernel(*refs):
    inputs, weight, share, blocks = refs[:7], refs[7], refs[8], refs[9 : 9 + CUTS]
    kept, refs = refs[9 + CUTS : 9 + 2 * CUTS], refs[9 + 2 * CUTS :]
    local, sems = refs[:7], refs[7]
    copies = [pltpu.make_async_copy(a, b, sems.at[i]) for i, (a, b) in enumerate(zip(inputs, local))]
    group, (place, _, _) = share.shape[1] // 3, here()
    for part in range(3):
        first = pl.multiple_of(part * (weight.shape[1] // 3) + place * group, group)
        copies.append(
            pltpu.make_async_copy(
                weight.at[:, pl.ds(first, group)],
                share.at[:, pl.ds(part * group, group)],
                sems.at[7 + part],
            )
        )
    for copy in copies:
        copy.start()
    for copy in copies[:7]:
        copy.wait()
    patches, rows, cols, row_table, col_table, segs, gain = local
    length = patches.shape[0]
    x = embedding(patches, rows, cols, row_table, col_table)
    centered = x - jnp.mean(x, axis=-1, keepdims=True)
    variance = jnp.mean(centered * centered, axis=-1, keepdims=True)
    normed = (centered * lax.rsqrt(variance + epsilon) * gain[...]).astype(jnp.bfloat16)
    labels = jnp.broadcast_to(segs[...].astype(jnp.float32), (PAD, length)).astype(jnp.bfloat16)
    cut = length // CUTS
    for i, block in enumerate(blocks):
        block[:cut, :] = normed[i * cut : (i + 1) * cut]
        block[cut:, :] = jnp.zeros((PAD, block.shape[1]), jnp.bfloat16)
        block[cut:, :cut] = labels[:, i * cut : (i + 1) * cut]
        copies.append(pltpu.make_async_copy(block, kept[i], sems.at[10 + i]))
        copies[-1].start()
    for copy in copies[7:]:
        copy.wait()


def matched(block, weights, columns):
    depth, length = weights[0].shape[0], block.shape[0] - PAD
    _, _, order = here()
    total = None
    for piece, weight in enumerate(weights):
        lanes = pl.ds(pl.multiple_of(order[piece] * depth, depth), depth)
        part = jnp.dot(
            block[:length, lanes], weight[:, columns], preferred_element_type=jnp.float32
        )
        total = part if total is None else total + part
    return total.astype(jnp.bfloat16)


def pick_kernel(*refs):
    away, two, block, one, sems = refs[:CUTS], refs[CUTS : 2 * CUTS], refs[-CUTS - 2], refs[-CUTS - 1 : -1], refs[-1]
    copies = [pltpu.make_async_copy(a, b, sems.at[i]) for i, (a, b) in enumerate(zip(away, one))]
    for copy in copies:
        copy.start()
    for copy in copies:
        copy.wait()
    pick(one, two, block)


def pick(one, two, block):
    _, own, _ = here()
    length = block.shape[0] - PAD
    cut = length // CUTS
    block[length:, :] = jnp.zeros((PAD, block.shape[1]), jnp.bfloat16)
    for i, (a, b) in enumerate(zip(one, two)):
        part = jnp.where(own, a[...], b[...])
        block[i * cut : (i + 1) * cut, :] = part[:cut]
        block[length:, i * cut : (i + 1) * cut] = part[cut:, :cut]


def keys_kernel(pieces, tile, *refs):
    if len(refs) == 2 + pieces:
        block, weights, kv_out = refs[0], refs[1:-1], refs[-1]
    else:
        weights, (block, kv_out) = refs[2 * CUTS : 2 * CUTS + pieces], refs[2 * CUTS + pieces :]
        pick(refs[:CUTS], refs[CUTS : 2 * CUTS], block)
    length, third = block.shape[0] - PAD, weights[0].shape[1] // 3
    kv_out[length:, :] = jnp.zeros((PAD, 2 * third), jnp.bfloat16)
    kv_out[length:, :length] = block[length:, :length]
    for first in range(0, 2 * third, tile):
        columns = slice(third + first, third + first + tile)
        kv_out[:length, first : first + tile] = matched(block, weights, columns)


def queries_kernel(slots, pieces, tile, scale, *refs):
    blocks, weights, outs = refs[:slots], refs[slots : slots + pieces], refs[slots + pieces :]
    for block, out in zip(blocks, outs):
        for first in range(0, out.shape[1], tile):
            columns = slice(first, first + tile)
            out[:, columns] = matched(block, weights, columns) * jnp.bfloat16(scale)


def attend_kernel(slots, slot, head, q, *refs):
    keys, (out, hot, gate) = refs[: 2 * slots], refs[2 * slots :]
    length, third = q.shape
    level = lax.broadcasted_iota(jnp.int32, (128, length), 0).astype(jnp.float32)
    for j, ref in enumerate(keys):
        match = ref[length : length + 1, :length].astype(jnp.float32) == level
        gate[pl.ds(j * length, length), :] = (
            jnp.where(match, 0.0, floor_score).T.astype(jnp.bfloat16)
        )
        if j == slot:
            hot[...] = jnp.where(match, 1.0, 0.0).T.astype(jnp.bfloat16)
    lane = lax.broadcasted_iota(jnp.int32, (length, 2 * head), 1)
    nt = (((1,), (1,)), ((), ()))
    ones = jnp.ones((length, 2 * head), jnp.bfloat16)

    def pair(index, carry):
        lanes = pl.ds(pl.multiple_of(index * 2 * head, 2 * head), 2 * head)
        values = pl.ds(pl.multiple_of(third + index * 2 * head, 2 * head), 2 * head)
        both = q[:, lanes]
        mixed = []
        for low in (True, False):
            mask = (lane < head) if low else (lane >= head)
            one = jnp.concatenate([jnp.where(mask, both, jnp.zeros_like(both)), hot[...]], axis=1)
            scores = [
                lax.dot_general(
                    one,
                    jnp.concatenate([ref[:length, lanes], gate[pl.ds(j * length, length), :]], axis=1),
                    nt,
                    preferred_element_type=jnp.float32,
                )
                for j, ref in enumerate(keys)
            ]
            highest = functools.reduce(
                jnp.maximum, [jnp.max(s, axis=-1, keepdims=True) for s in scores]
            )
            product = sum(
                jnp.dot(
                    jnp.exp(s - highest).astype(jnp.bfloat16),
                    jnp.concatenate([ref[:length, values], ones], axis=1),
                    preferred_element_type=jnp.float32,
                )
                for s, ref in zip(scores, keys)
            )
            mixed.append(product[:, : 2 * head] / product[:, 2 * head :])
        out[:, lanes] = jnp.where(lane < head, mixed[0], mixed[1]).astype(jnp.bfloat16)
        return carry

    lax.fori_loop(0, third // (2 * head), pair, 0, unroll=True)


def first_kernel(slots, pieces, *refs):
    inputs, refs = refs[:5], refs[5:]
    contexts, weights = refs[: slots - 1], refs[slots - 1 : slots - 1 + pieces]
    out, kept = refs[slots - 1 + pieces : slots + 1 + pieces]
    local, sems = refs[slots + 1 + pieces : -1], refs[-1]
    copies = [pltpu.make_async_copy(a, b, sems.at[i]) for i, (a, b) in enumerate(zip(inputs, local))]
    for copy in copies:
        copy.start()
    for copy in copies:
        copy.wait()
    out[...] = embedding(*local)
    width, span = kept.shape[0], weights[0].shape[1]
    place, _, order = here()
    rows = [
        pl.ds(pl.multiple_of(lax.rem(place + j, slots) * width, width), width) for j in range(slots)
    ]
    for piece, weight in enumerate(weights):
        lanes = pl.ds(pl.multiple_of(order[piece] * span, span), span)
        kept[:, lanes] = weight[rows[-1], :]
        for context, row in zip(contexts, rows):
            out[:, lanes] += jnp.dot(context[...], weight[row, :], preferred_element_type=jnp.float32)


def last_kernel(base, context, weight, out):
    out[...] = (
        base[...] + jnp.dot(context[...], weight[...], preferred_element_type=jnp.float32)
    ).astype(out.dtype)


def body(
    patches, segment_ids, patch_rows, patch_cols, row_table, col_table, norm_gain, qkv_weight, out_weight
):
    n, lanes = lax.axis_size("ctx"), lax.axis_size("fsdp")
    half, chips = n // 2, lanes // 2
    own = lax.axis_index("ctx") // half == lax.axis_index("fsdp") % 2
    length, model = patches.shape[1:]
    head = model // HEADS
    group = model // half

    def spread(j):
        pairs = []
        for a in range(n):
            for b in range(lanes):
                core = b % 2
                to = core * half + (a % half + j) % half
                to_core = core if a // half == core else 1 - core
                pairs.append((a * lanes + b, to * lanes + b - core + to_core))
        return pairs

    def around(j, near):
        return [
            (a * lanes + b, (a - a % half + (a % half + j) % half) * lanes + b)
            for a in range(n)
            for b in range(lanes)
            if (a // half == b % 2) == near
        ]

    def moves(near, far):
        holders = {p for p, _ in around(0, True)}
        return [p for p in near if p[0] in holders] + [p for p in far if p[0] not in holders]

    def send_cuts(values, pairs):
        return [send(value, pairs) for value in values]

    def send(value, pairs):
        return lax.ppermute(value, ("ctx", "fsdp"), pairs)

    def along(value, by):
        return lax.ppermute(value, "fsdp", [(i, (i + 2 * by) % lanes) for i in range(lanes)])

    def partner(value):
        return lax.ppermute(value, "fsdp", [(i, i ^ 1) for i in range(lanes)])

    def gather(piece):
        own = [piece] + [along(piece, by) for by in range(1, chips)]
        return own + [partner(p) for p in own]

    depth = qkv_weight.shape[0]
    shape = jax.ShapeDtypeStruct
    inputs = (
        patches[0],
        patch_rows,
        patch_cols,
        row_table,
        col_table,
        segment_ids,
        norm_gain.reshape(1, model),
    )
    kept = [pltpu.with_memory_space_constraint(a, pltpu.HBM) for a in (*inputs, qkv_weight)]
    local = [pltpu.VMEM(a.shape, a.dtype) for a in inputs]
    share, *made = call(
        embed_kernel,
        [
            shape((depth, 3 * group), jnp.bfloat16),
            *[shape((length // CUTS + PAD, model), jnp.bfloat16)] * (2 * CUTS),
        ],
        kept,
        [HB] * 8,
        4 * length * row_table.shape[0] * model,
        scratch=local + [pltpu.SemaphoreType.DMA((10 + CUTS,))],
        away=CUTS,
    )
    block, parked = made[:CUTS], made[CUTS:]
    weights = gather(share)
    out_weights = gather(out_weight)
    first = send_cuts(block, moves(around(1 % half, True), spread(0)))
    whole = shape((length + PAD, model), jnp.bfloat16)
    (picked,) = call(
        pick_kernel,
        [whole],
        (*parked, *first),
        [HB] * CUTS + [VM] * CUTS,
        0,
        scratch=[pltpu.VMEM(a.shape, a.dtype) for a in block] + [pltpu.SemaphoreType.DMA((CUTS,))],
    )
    blocks = [(picked,), (*first, *send_cuts(first, around(1, False)))]
    for j in range(2, half):
        held = [jnp.where(own, a, b) for a, b in zip(block, first)]
        held = send_cuts(held, around(j, True) + around(j, False))
        blocks.append((*held, *held))
    tile = min(group, 256)
    slots, keys = [], []
    for j, ways in enumerate(blocks):
        *slot, kv = call(
            functools.partial(keys_kernel, lanes, tile),
            [whole] * (j > 0) + [shape((length + PAD, 2 * group), jnp.bfloat16)],
            (*ways, *weights),
            [VM] * (len(ways) + lanes),
            4 * length * model * group,
        )
        slots += slot or [picked]
        keys.append(kv)
    queries = call(
        functools.partial(queries_kernel, half, lanes, tile, 1.0 / head**0.5),
        [shape((length, group), jnp.bfloat16)] * half,
        (*slots, *weights),
        [VM] * (half + lanes),
        2 * half * length * model * group,
    )
    keys += [partner(kv) for kv in keys]
    contexts = []
    for j in range(half):
        (context,) = call(
            functools.partial(attend_kernel, half, j, head),
            [shape((length, group), jnp.bfloat16)],
            (queries[j], *keys),
            [VM] * (1 + 2 * half),
            8 * length * half * length * 2 * group,
            scratch=[
                pltpu.VMEM((length, 128), jnp.bfloat16),
                pltpu.VMEM((2 * half * length, 128), jnp.bfloat16),
            ],
        )
        contexts.append(send(context, [(b, a) for a, b in spread(j)]))
    base, kept_rows = call(
        functools.partial(first_kernel, half, lanes),
        [shape((length, model), jnp.float32), shape((group, model), jnp.bfloat16)],
        (*kept[:5], *contexts[:-1], *out_weights),
        [HB] * 5 + [VM] * (half - 1 + lanes),
        2 * length * model * (model - group),
        scratch=local[:5] + [pltpu.SemaphoreType.DMA((5,))],
    )
    (encoded,) = call(
        last_kernel,
        [shape((length, model), jnp.bfloat16)],
        (base, contexts[-1], kept_rows),
        [VM] * 3,
        2 * length * model * group,
    )
    return encoded[None]


def solution(mesh):
    return jax.shard_map(
        body,
        mesh=mesh,
        in_specs=(
            P(("groups", "fsdp"), "ctx", None),
            P(("groups", "fsdp"), "ctx"),
            P(("groups", "fsdp"), "ctx"),
            P(("groups", "fsdp"), "ctx"),
            P(),
            P(),
            P(),
            P("fsdp", None),
            P(None, "fsdp"),
        ),
        out_specs=P(("groups", "fsdp"), "ctx", None),
        check_vma=False,
    )
```

```python
import functools

import jax
import jax.numpy as jnp
from jax import lax
from jax.experimental import pallas as pl
from jax.experimental.pallas import tpu as pltpu
from jax.sharding import PartitionSpec as P


HEADS = 16
floor_score = -1e30
epsilon = 1e-06
VM = pl.BlockSpec(memory_space=pltpu.VMEM)
PAD = 16
CUTS = 2
FIRST = 10


HB = pl.BlockSpec(memory_space=pltpu.HBM)


def here():
    half, lanes = lax.axis_size("ctx") // 2, lax.axis_size("fsdp")
    z, f = lax.axis_index("ctx"), lax.axis_index("fsdp")
    chips, core = lanes // 2, lax.rem(f, 2)
    sources = [2 * lax.rem(lax.div(f, 2) + chips - by, chips) + core for by in range(chips)]
    order = sources + [s + 1 - 2 * core for s in sources]
    return lax.rem(z, half), lax.div(z, half) == core, order


def cut(length):
    first = length * FIRST // 16
    return (0, first), (first, length)


def call(kernel, outs, args, specs, flops, scratch=()):
    moved = sum(a.size * a.dtype.itemsize for a in (*args, *outs))
    return pl.pallas_call(
        kernel,
        out_shape=outs,
        in_specs=specs,
        out_specs=[VM] * len(outs),
        scratch_shapes=scratch,
        compiler_params=pltpu.CompilerParams(vmem_limit_bytes=16 << 20),
        cost_estimate=pl.CostEstimate(flops=flops, bytes_accessed=moved, transcendentals=0),
    )(*args)


def embedding(patches, rows, cols, row_table, col_table):
    length, grid = patches.shape[0], row_table.shape[0]
    level = lax.broadcasted_iota(jnp.int32, (grid, length), 0)
    row_hot = jnp.where(rows[...] == level, 1.0, 0.0).T.astype(jnp.bfloat16)
    col_hot = jnp.where(cols[...] == level, 1.0, 0.0).T.astype(jnp.bfloat16)
    return (
        patches[...].astype(jnp.float32)
        + jnp.dot(row_hot, row_table[...], preferred_element_type=jnp.float32)
        + jnp.dot(col_hot, col_table[...], preferred_element_type=jnp.float32)
    )


def embed_kernel(*refs):
    inputs, weight, share_q, share_kv, blocks = refs[:7], refs[7], refs[8], refs[9], refs[10 : 10 + CUTS]
    local, sems = refs[10 + CUTS : 17 + CUTS], refs[17 + CUTS]
    copies = [pltpu.make_async_copy(a, b, sems.at[i]) for i, (a, b) in enumerate(zip(inputs, local))]
    group, (place, _, _) = share_q.shape[1], here()
    for part in range(3):
        first = pl.multiple_of(part * (weight.shape[1] // 3) + place * group, group)
        copies.append(
            pltpu.make_async_copy(
                weight.at[:, pl.ds(first, group)],
                share_kv.at[:, pl.ds((part - 1) * group, group)] if part else share_q,
                sems.at[7 + part],
            )
        )
    for copy in copies:
        copy.start()
    for copy in copies[:7]:
        copy.wait()
    patches, rows, cols, row_table, col_table, segs, gain = local
    length = patches.shape[0]
    x = embedding(patches, rows, cols, row_table, col_table)
    centered = x - jnp.mean(x, axis=-1, keepdims=True)
    variance = jnp.mean(centered * centered, axis=-1, keepdims=True)
    normed = (centered * lax.rsqrt(variance + epsilon) * gain[...]).astype(jnp.bfloat16)
    labels = jnp.broadcast_to(segs[...].astype(jnp.float32), (PAD, length)).astype(jnp.bfloat16)
    for block, (start, stop) in zip(blocks, cut(length)):
        rows = stop - start
        block[:rows, :] = normed[start:stop]
        block[rows:, :] = jnp.zeros((PAD, block.shape[1]), jnp.bfloat16)
        block[rows:, :length] = labels
    for copy in copies[7:]:
        copy.wait()


def matched(block, weights, columns):
    depth, length = weights[0].shape[0], block.shape[0] - PAD
    _, _, order = here()
    total = None
    for piece, weight in enumerate(weights):
        lanes = pl.ds(pl.multiple_of(order[piece] * depth, depth), depth)
        part = jnp.dot(
            block[:length, lanes], weight[:, columns], preferred_element_type=jnp.float32
        )
        total = part if total is None else total + part
    return total.astype(jnp.bfloat16)


def pick_kernel(one, two, out):
    _, own, _ = here()
    out[...] = jnp.where(own, one[...], two[...])


def keys_kernel(pieces, ways, tile, *refs):
    _, own, _ = here()
    weights, (block, kv_out) = refs[-2 - pieces : -2], refs[-2:]
    at = 0
    for count, (start, stop) in zip(ways, cut(block.shape[0] - PAD)):
        part = refs[at][...]
        if count == 2:
            part = jnp.where(own, part, refs[at + 1][...])
        block[start:stop, :] = part[: stop - start]
        if start == 0:
            block[block.shape[0] - PAD :, :] = part[stop:]
        at += count
    length, third = block.shape[0] - PAD, weights[0].shape[1] // 2
    kv_out[length:, :] = jnp.zeros((PAD, 2 * third), jnp.bfloat16)
    kv_out[length:, :length] = block[length:, :length]
    for first in range(0, 2 * third, tile):
        columns = slice(first, first + tile)
        kv_out[:length, first : first + tile] = matched(block, weights, columns)


def queries_kernel(slots, pieces, tile, scale, *refs):
    blocks, weights, outs = refs[:slots], refs[slots : slots + pieces], refs[slots + pieces :]
    for block, out in zip(blocks, outs):
        for first in range(0, out.shape[1], tile):
            columns = slice(first, first + tile)
            out[:, columns] = matched(block, weights, columns) * jnp.bfloat16(scale)


def attend_kernel(slots, slot, head, q, *refs):
    keys, (out, hot, gate) = refs[: 2 * slots], refs[2 * slots :]
    length, third = q.shape
    level = lax.broadcasted_iota(jnp.int32, (128, length), 0).astype(jnp.float32)
    for j, ref in enumerate(keys):
        match = ref[length : length + 1, :length].astype(jnp.float32) == level
        gate[pl.ds(j * length, length), :] = (
            jnp.where(match, 0.0, floor_score).T.astype(jnp.bfloat16)
        )
        if j == slot:
            hot[...] = jnp.where(match, 1.0, 0.0).T.astype(jnp.bfloat16)
    lane = lax.broadcasted_iota(jnp.int32, (length, 2 * head), 1)
    nt = (((1,), (1,)), ((), ()))
    ones = jnp.ones((length, 2 * head), jnp.bfloat16)

    def pair(index, carry):
        lanes = pl.ds(pl.multiple_of(index * 2 * head, 2 * head), 2 * head)
        values = pl.ds(pl.multiple_of(third + index * 2 * head, 2 * head), 2 * head)
        both = q[:, lanes]
        mixed = []
        for low in (True, False):
            mask = (lane < head) if low else (lane >= head)
            one = jnp.concatenate([jnp.where(mask, both, jnp.zeros_like(both)), hot[...]], axis=1)
            scores = [
                lax.dot_general(
                    one,
                    jnp.concatenate([ref[:length, lanes], gate[pl.ds(j * length, length), :]], axis=1),
                    nt,
                    preferred_element_type=jnp.float32,
                )
                for j, ref in enumerate(keys)
            ]
            highest = functools.reduce(
                jnp.maximum, [jnp.max(s, axis=-1, keepdims=True) for s in scores]
            )
            product = sum(
                jnp.dot(
                    jnp.exp(s - highest).astype(jnp.bfloat16),
                    jnp.concatenate([ref[:length, values], ones], axis=1),
                    preferred_element_type=jnp.float32,
                )
                for s, ref in zip(scores, keys)
            )
            mixed.append(product[:, : 2 * head] / product[:, 2 * head :])
        out[:, lanes] = jnp.where(lane < head, mixed[0], mixed[1]).astype(jnp.bfloat16)
        return carry

    lax.fori_loop(0, third // (2 * head), pair, 0, unroll=True)


def first_kernel(slots, pieces, *refs):
    inputs, refs = refs[:5], refs[5:]
    contexts, weights = refs[: slots - 1], refs[slots - 1 : slots - 1 + pieces]
    out, kept = refs[slots - 1 + pieces : slots + 1 + pieces]
    local, sems = refs[slots + 1 + pieces : -1], refs[-1]
    copies = [pltpu.make_async_copy(a, b, sems.at[i]) for i, (a, b) in enumerate(zip(inputs, local))]
    for copy in copies:
        copy.start()
    for copy in copies:
        copy.wait()
    out[...] = embedding(*local)
    width, span = kept.shape[0], weights[0].shape[1]
    place, _, order = here()
    rows = [
        pl.ds(pl.multiple_of(lax.rem(place + j, slots) * width, width), width) for j in range(slots)
    ]
    for piece, weight in enumerate(weights):
        lanes = pl.ds(pl.multiple_of(order[piece] * span, span), span)
        kept[:, lanes] = weight[rows[-1], :]
        for context, row in zip(contexts, rows):
            out[:, lanes] += jnp.dot(context[...], weight[row, :], preferred_element_type=jnp.float32)


def last_kernel(base, context, weight, out):
    out[...] = (
        base[...] + jnp.dot(context[...], weight[...], preferred_element_type=jnp.float32)
    ).astype(out.dtype)


def body(
    patches, segment_ids, patch_rows, patch_cols, row_table, col_table, norm_gain, qkv_weight, out_weight
):
    n, lanes = lax.axis_size("ctx"), lax.axis_size("fsdp")
    half, chips = n // 2, lanes // 2
    own = lax.axis_index("ctx") // half == lax.axis_index("fsdp") % 2
    length, model = patches.shape[1:]
    head = model // HEADS
    group = model // half

    def spread(j):
        pairs = []
        for a in range(n):
            for b in range(lanes):
                core = b % 2
                to = core * half + (a % half + j) % half
                to_core = core if a // half == core else 1 - core
                pairs.append((a * lanes + b, to * lanes + b - core + to_core))
        return pairs

    def around(j, near):
        return [
            (a * lanes + b, (a - a % half + (a % half + j) % half) * lanes + b)
            for a in range(n)
            for b in range(lanes)
            if (a // half == b % 2) == near
        ]

    def moves(near, far):
        holders = {p for p, _ in around(0, True)}
        return [p for p in near if p[0] in holders] + [p for p in far if p[0] not in holders]

    def send_cuts(values, pairs):
        return [send(value, pairs) for value in values]

    def send(value, pairs):
        return lax.ppermute(value, ("ctx", "fsdp"), pairs)

    def along(value, by):
        return lax.ppermute(value, "fsdp", [(i, (i + 2 * by) % lanes) for i in range(lanes)])

    def partner(value):
        return lax.ppermute(value, "fsdp", [(i, i ^ 1) for i in range(lanes)])

    def gather(piece):
        own = [piece] + [along(piece, by) for by in range(1, chips)]
        return own + [partner(p) for p in own]

    depth = qkv_weight.shape[0]
    shape = jax.ShapeDtypeStruct
    inputs = (
        patches[0],
        patch_rows,
        patch_cols,
        row_table,
        col_table,
        segment_ids,
        norm_gain.reshape(1, model),
    )
    kept = [pltpu.with_memory_space_constraint(a, pltpu.HBM) for a in (*inputs, qkv_weight)]
    local = [pltpu.VMEM(a.shape, a.dtype) for a in inputs]
    share_q, share_kv, *block = call(
        embed_kernel,
        [
            shape((depth, group), jnp.bfloat16),
            shape((depth, 2 * group), jnp.bfloat16),
            *[shape((b - a + PAD, model), jnp.bfloat16) for a, b in cut(length)],
        ],
        kept,
        [HB] * 8,
        4 * length * row_table.shape[0] * model,
        scratch=local + [pltpu.SemaphoreType.DMA((10,))],
    )
    kv_weights, q_weights = gather(share_kv), gather(share_q)
    out_weights = gather(out_weight)
    first = send_cuts(block, moves(around(1 % half, True), spread(0)))
    whole = shape((length + PAD, model), jnp.bfloat16)
    picked = call(pick_kernel, [shape(block[0].shape, jnp.bfloat16)], (block[0], first[0]), [VM] * 2, 0)
    relayed = send_cuts(first, around(1, False))
    blocks = [[picked, *zip(block[1:], first[1:])], list(zip(first, relayed))]
    for j in range(2, half):
        held = [jnp.where(own, a, b) for a, b in zip(block, first)]
        held = send_cuts(held, around(j, True) + around(j, False))
        blocks.append([[h] for h in held])
    tile = min(group, 256)
    slots, keys = [], []
    for ways in blocks:
        ways, parts = tuple(len(w) for w in ways), [p for w in ways for p in w]
        slot, kv = call(
            functools.partial(keys_kernel, lanes, ways, tile),
            [whole, shape((length + PAD, 2 * group), jnp.bfloat16)],
            (*parts, *kv_weights),
            [VM] * (len(parts) + lanes),
            4 * length * model * group,
        )
        slots.append(slot)
        keys.append(kv)
    queries = call(
        functools.partial(queries_kernel, half, lanes, tile, 1.0 / head**0.5),
        [shape((length, group), jnp.bfloat16)] * half,
        (*slots, *q_weights),
        [VM] * (half + lanes),
        2 * half * length * model * group,
    )
    keys += [partner(kv) for kv in keys]
    contexts = []
    for j in range(half):
        (context,) = call(
            functools.partial(attend_kernel, half, j, head),
            [shape((length, group), jnp.bfloat16)],
            (queries[j], *keys),
            [VM] * (1 + 2 * half),
            8 * length * half * length * 2 * group,
            scratch=[
                pltpu.VMEM((length, 128), jnp.bfloat16),
                pltpu.VMEM((2 * half * length, 128), jnp.bfloat16),
            ],
        )
        contexts.append(send(context, [(b, a) for a, b in spread(j)]))
    base, kept_rows = call(
        functools.partial(first_kernel, half, lanes),
        [shape((length, model), jnp.float32), shape((group, model), jnp.bfloat16)],
        (*kept[:5], *contexts[:-1], *out_weights),
        [HB] * 5 + [VM] * (half - 1 + lanes),
        2 * length * model * (model - group),
        scratch=local[:5] + [pltpu.SemaphoreType.DMA((5,))],
    )
    (encoded,) = call(
        last_kernel,
        [shape((length, model), jnp.bfloat16)],
        (base, contexts[-1], kept_rows),
        [VM] * 3,
        2 * length * model * group,
    )
    return encoded[None]


def solution(mesh):
    return jax.shard_map(
        body,
        mesh=mesh,
        in_specs=(
            P(("groups", "fsdp"), "ctx", None),
            P(("groups", "fsdp"), "ctx"),
            P(("groups", "fsdp"), "ctx"),
            P(("groups", "fsdp"), "ctx"),
            P(),
            P(),
            P(),
            P("fsdp", None),
            P(None, "fsdp"),
        ),
        out_specs=P(("groups", "fsdp"), "ctx", None),
        check_vma=False,
    )
```

```python
import functools

import jax
import jax.numpy as jnp
from jax import lax
from jax.experimental import pallas as pl
from jax.experimental.pallas import tpu as pltpu
from jax.sharding import PartitionSpec as P


HEADS = 16
floor_score = -1e30
epsilon = 1e-06
VM = pl.BlockSpec(memory_space=pltpu.VMEM)
PAD = 16
CUTS = 2
FIRST = 10


HB = pl.BlockSpec(memory_space=pltpu.HBM)


def here():
    half, lanes = lax.axis_size("ctx") // 2, lax.axis_size("fsdp")
    z, f = lax.axis_index("ctx"), lax.axis_index("fsdp")
    chips, core = lanes // 2, lax.rem(f, 2)
    sources = [2 * lax.rem(lax.div(f, 2) + chips - by, chips) + core for by in range(chips)]
    order = sources + [s + 1 - 2 * core for s in sources]
    return lax.rem(z, half), lax.div(z, half) == core, order


def cut(length):
    first = length * FIRST // 16
    return (0, first), (first, length)


def call(kernel, outs, args, specs, flops, scratch=()):
    moved = sum(a.size * a.dtype.itemsize for a in (*args, *outs))
    return pl.pallas_call(
        kernel,
        out_shape=outs,
        in_specs=specs,
        out_specs=[VM] * len(outs),
        scratch_shapes=scratch,
        compiler_params=pltpu.CompilerParams(vmem_limit_bytes=16 << 20),
        cost_estimate=pl.CostEstimate(flops=flops, bytes_accessed=moved, transcendentals=0),
    )(*args)


def embedding(patches, rows, cols, row_table, col_table):
    length, grid = patches.shape[0], row_table.shape[0]
    level = lax.broadcasted_iota(jnp.int32, (grid, length), 0)
    row_hot = jnp.where(rows[...] == level, 1.0, 0.0).T.astype(jnp.bfloat16)
    col_hot = jnp.where(cols[...] == level, 1.0, 0.0).T.astype(jnp.bfloat16)
    return (
        patches[...].astype(jnp.float32)
        + jnp.dot(row_hot, row_table[...], preferred_element_type=jnp.float32)
        + jnp.dot(col_hot, col_table[...], preferred_element_type=jnp.float32)
    )


def embed_kernel(*refs):
    inputs, weight, share_q, share_kv, blocks = refs[:7], refs[7], refs[8], refs[9], refs[10 : 10 + CUTS]
    local, sems = refs[10 + CUTS : 17 + CUTS], refs[17 + CUTS]
    copies = [pltpu.make_async_copy(a, b, sems.at[i]) for i, (a, b) in enumerate(zip(inputs, local))]
    group, (place, _, _) = share_q.shape[1], here()
    for part in range(3):
        first = pl.multiple_of(part * (weight.shape[1] // 3) + place * group, group)
        copies.append(
            pltpu.make_async_copy(
                weight.at[:, pl.ds(first, group)],
                share_kv.at[:, pl.ds((part - 1) * group, group)] if part else share_q,
                sems.at[7 + part],
            )
        )
    for copy in copies:
        copy.start()
    for copy in copies[:7]:
        copy.wait()
    patches, rows, cols, row_table, col_table, segs, gain = local
    length = patches.shape[0]
    x = embedding(patches, rows, cols, row_table, col_table)
    centered = x - jnp.mean(x, axis=-1, keepdims=True)
    variance = jnp.mean(centered * centered, axis=-1, keepdims=True)
    normed = (centered * lax.rsqrt(variance + epsilon) * gain[...]).astype(jnp.bfloat16)
    labels = jnp.broadcast_to(segs[...].astype(jnp.float32), (PAD, length)).astype(jnp.bfloat16)
    for block, (start, stop) in zip(blocks, cut(length)):
        rows = stop - start
        block[:rows, :] = normed[start:stop]
        block[rows:, :] = jnp.zeros((PAD, block.shape[1]), jnp.bfloat16)
        block[rows:, :length] = labels
    for copy in copies[7:]:
        copy.wait()


def matched(block, weights, columns):
    depth, length = weights[0].shape[0], block.shape[0] - PAD
    _, _, order = here()
    total = None
    for piece, weight in enumerate(weights):
        lanes = pl.ds(pl.multiple_of(order[piece] * depth, depth), depth)
        part = jnp.dot(
            block[:length, lanes], weight[:, columns], preferred_element_type=jnp.float32
        )
        total = part if total is None else total + part
    return total.astype(jnp.bfloat16)


def pick_kernel(one, two, out):
    _, own, _ = here()
    out[...] = jnp.where(own, one[...], two[...])


def keys_kernel(pieces, ways, tile, *refs):
    _, own, _ = here()
    weights, (block, kv_out) = refs[-2 - pieces : -2], refs[-2:]
    at = 0
    for count, (start, stop) in zip(ways, cut(block.shape[0] - PAD)):
        part = refs[at][...]
        if count == 2:
            part = jnp.where(own, part, refs[at + 1][...])
        block[start:stop, :] = part[: stop - start]
        if start == 0:
            block[block.shape[0] - PAD :, :] = part[stop:]
        at += count
    length, third = block.shape[0] - PAD, weights[0].shape[1] // 2
    kv_out[length:, :] = jnp.zeros((PAD, 2 * third), jnp.bfloat16)
    kv_out[length:, :length] = block[length:, :length]
    for first in range(0, 2 * third, tile):
        columns = slice(first, first + tile)
        kv_out[:length, first : first + tile] = matched(block, weights, columns)


def queries_kernel(slots, pieces, tile, scale, *refs):
    blocks, weights, outs = refs[:slots], refs[slots : slots + pieces], refs[slots + pieces :]
    for block, out in zip(blocks, outs):
        for first in range(0, out.shape[1], tile):
            columns = slice(first, first + tile)
            out[:, columns] = matched(block, weights, columns) * jnp.bfloat16(scale)


def attend_kernel(count, head, resume, finish, q, owner, *refs):
    keys, refs = refs[:count], refs[count:]
    before, refs = (refs[:3], refs[3:]) if resume else (None, refs)
    outs, (hot, gate) = refs[:-2], refs[-2:]
    length, third = q.shape
    level = lax.broadcasted_iota(jnp.int32, (128, length), 0).astype(jnp.float32)

    def match(ref):
        return ref[length : length + 1, :length].astype(jnp.float32) == level

    hot[...] = jnp.where(match(owner), 1.0, 0.0).T.astype(jnp.bfloat16)
    for j, ref in enumerate(keys):
        gate[pl.ds(j * length, length), :] = (
            jnp.where(match(ref), 0.0, floor_score).T.astype(jnp.bfloat16)
        )
    span = 2 * head
    lane = lax.broadcasted_iota(jnp.int32, (length, span), 1)
    nt = (((1,), (1,)), ((), ()))
    ones = jnp.ones((length, span), jnp.bfloat16)

    def pair(index, carry):
        lanes = pl.ds(pl.multiple_of(index * span, span), span)
        values = pl.ds(pl.multiple_of(third + index * span, span), span)
        both = q[:, lanes]
        if resume:
            held = [ref[:, lanes] for ref in before[:2]]
        results = []
        for which, low in enumerate((0, head)):
            own = pl.ds(pl.multiple_of((2 * index + which) * span, span), span)
            mask = (lane >= low) & (lane < low + head)
            one = jnp.concatenate([jnp.where(mask, both, jnp.zeros_like(both)), hot[...]], axis=1)
            scores = [
                lax.dot_general(
                    one,
                    jnp.concatenate([ref[:length, lanes], gate[pl.ds(j * length, length), :]], axis=1),
                    nt,
                    preferred_element_type=jnp.float32,
                )
                for j, ref in enumerate(keys)
            ]
            highest = functools.reduce(
                jnp.maximum, [jnp.max(s, axis=-1, keepdims=True) for s in scores]
            )
            highest = jnp.broadcast_to(highest, (length, span))
            if resume:
                earlier = before[2][:, own]
                highest = jnp.maximum(highest, earlier)
            wide = jnp.concatenate([highest] * (length // span), axis=1)
            product = sum(
                jnp.dot(
                    jnp.exp(s - wide).astype(jnp.bfloat16),
                    jnp.concatenate([ref[:length, values], ones], axis=1),
                    preferred_element_type=jnp.float32,
                )
                for s, ref in zip(scores, keys)
            )
            mixed, total = product[:, :span], product[:, span:]
            if resume:
                factor = jnp.exp(earlier - highest)
                mixed, total = mixed + held[0] * factor, total + held[1] * factor
            if finish:
                results.append((mixed / total,))
            else:
                results.append((mixed, total))
                outs[2][:, own] = highest
        for out, one, two in zip(outs, *results):
            out[:, lanes] = jnp.where(lane < head, one, two).astype(out.dtype)
        return carry

    lax.fori_loop(0, third // span, pair, 0, unroll=True)


def first_kernel(slots, pieces, *refs):
    inputs, refs = refs[:5], refs[5:]
    contexts, weights = refs[: slots - 1], refs[slots - 1 : slots - 1 + pieces]
    out, kept = refs[slots - 1 + pieces : slots + 1 + pieces]
    local, sems = refs[slots + 1 + pieces : -1], refs[-1]
    copies = [pltpu.make_async_copy(a, b, sems.at[i]) for i, (a, b) in enumerate(zip(inputs, local))]
    for copy in copies:
        copy.start()
    for copy in copies:
        copy.wait()
    out[...] = embedding(*local)
    width, span = kept.shape[0], weights[0].shape[1]
    place, _, order = here()
    rows = [
        pl.ds(pl.multiple_of(lax.rem(place + j, slots) * width, width), width) for j in range(slots)
    ]
    for piece, weight in enumerate(weights):
        lanes = pl.ds(pl.multiple_of(order[piece] * span, span), span)
        kept[:, lanes] = weight[rows[-1], :]
        for context, row in zip(contexts, rows):
            out[:, lanes] += jnp.dot(context[...], weight[row, :], preferred_element_type=jnp.float32)


def last_kernel(base, context, weight, out):
    out[...] = (
        base[...] + jnp.dot(context[...], weight[...], preferred_element_type=jnp.float32)
    ).astype(out.dtype)


def body(
    patches, segment_ids, patch_rows, patch_cols, row_table, col_table, norm_gain, qkv_weight, out_weight
):
    n, lanes = lax.axis_size("ctx"), lax.axis_size("fsdp")
    half, chips = n // 2, lanes // 2
    own = lax.axis_index("ctx") // half == lax.axis_index("fsdp") % 2
    length, model = patches.shape[1:]
    head = model // HEADS
    group = model // half

    def spread(j):
        pairs = []
        for a in range(n):
            for b in range(lanes):
                core = b % 2
                to = core * half + (a % half + j) % half
                to_core = core if a // half == core else 1 - core
                pairs.append((a * lanes + b, to * lanes + b - core + to_core))
        return pairs

    def around(j, near):
        return [
            (a * lanes + b, (a - a % half + (a % half + j) % half) * lanes + b)
            for a in range(n)
            for b in range(lanes)
            if (a // half == b % 2) == near
        ]

    def moves(near, far):
        holders = {p for p, _ in around(0, True)}
        return [p for p in near if p[0] in holders] + [p for p in far if p[0] not in holders]

    def send_cuts(values, pairs):
        return [send(value, pairs) for value in values]

    def send(value, pairs):
        return lax.ppermute(value, ("ctx", "fsdp"), pairs)

    def along(value, by):
        return lax.ppermute(value, "fsdp", [(i, (i + 2 * by) % lanes) for i in range(lanes)])

    def partner(value):
        return lax.ppermute(value, "fsdp", [(i, i ^ 1) for i in range(lanes)])

    def gather(piece):
        own = [piece] + [along(piece, by) for by in range(1, chips)]
        return own + [partner(p) for p in own]

    depth = qkv_weight.shape[0]
    shape = jax.ShapeDtypeStruct
    inputs = (
        patches[0],
        patch_rows,
        patch_cols,
        row_table,
        col_table,
        segment_ids,
        norm_gain.reshape(1, model),
    )
    kept = [pltpu.with_memory_space_constraint(a, pltpu.HBM) for a in (*inputs, qkv_weight)]
    local = [pltpu.VMEM(a.shape, a.dtype) for a in inputs]
    share_q, share_kv, *block = call(
        embed_kernel,
        [
            shape((depth, group), jnp.bfloat16),
            shape((depth, 2 * group), jnp.bfloat16),
            *[shape((b - a + PAD, model), jnp.bfloat16) for a, b in cut(length)],
        ],
        kept,
        [HB] * 8,
        4 * length * row_table.shape[0] * model,
        scratch=local + [pltpu.SemaphoreType.DMA((10,))],
    )
    kv_weights, q_weights = gather(share_kv), gather(share_q)
    out_weights = gather(out_weight)
    first = send_cuts(block, moves(around(1 % half, True), spread(0)))
    whole = shape((length + PAD, model), jnp.bfloat16)
    picked = call(pick_kernel, [shape(block[0].shape, jnp.bfloat16)], (block[0], first[0]), [VM] * 2, 0)
    relayed = send_cuts(first, around(1, False))
    blocks = [[picked, *zip(block[1:], first[1:])], list(zip(first, relayed))]
    for j in range(2, half):
        held = [jnp.where(own, a, b) for a, b in zip(block, first)]
        held = send_cuts(held, around(j, True) + around(j, False))
        blocks.append([[h] for h in held])
    tile = min(group, 256)
    slots, keys = [], []
    for ways in blocks:
        ways, parts = tuple(len(w) for w in ways), [p for w in ways for p in w]
        slot, kv = call(
            functools.partial(keys_kernel, lanes, ways, tile),
            [whole, shape((length + PAD, 2 * group), jnp.bfloat16)],
            (*parts, *kv_weights),
            [VM] * (len(parts) + lanes),
            4 * length * model * group,
        )
        slots.append(slot)
        keys.append(kv)
    queries = call(
        functools.partial(queries_kernel, half, lanes, tile, 1.0 / head**0.5),
        [shape((length, group), jnp.bfloat16)] * half,
        (*slots, *q_weights),
        [VM] * (half + lanes),
        2 * half * length * model * group,
    )
    keys += [partner(kv) for kv in keys]
    context = shape((length, group), jnp.bfloat16)

    def attend(slot, blocks, held, outs):
        return call(
            functools.partial(attend_kernel, len(blocks), head, len(held) > 0, len(outs) == 1),
            outs,
            (queries[slot], keys[slot], *blocks, *held),
            [VM] * (2 + len(blocks) + len(held)),
            8 * length * len(blocks) * length * group,
            scratch=[
                pltpu.VMEM((length, 128), jnp.bfloat16),
                pltpu.VMEM((len(blocks) * length, 128), jnp.bfloat16),
            ],
        )

    late = [keys[half - 1], keys[-1]]
    state = shape((length, group), jnp.float32)
    wide = shape((length, 2 * group), jnp.float32)
    held = attend(0, keys[: half - 1] + keys[half:-1], [], [state, state, wide])
    contexts = []
    for j in range(half):
        (mixed,) = attend(j, keys if j else late, () if j else held, [context])
        contexts.append(send(mixed, [(b, a) for a, b in spread(j)]))
    base, kept_rows = call(
        functools.partial(first_kernel, half, lanes),
        [shape((length, model), jnp.float32), shape((group, model), jnp.bfloat16)],
        (*kept[:5], *contexts[:-1], *out_weights),
        [HB] * 5 + [VM] * (half - 1 + lanes),
        2 * length * model * (model - group),
        scratch=local[:5] + [pltpu.SemaphoreType.DMA((5,))],
    )
    (encoded,) = call(
        last_kernel,
        [shape((length, model), jnp.bfloat16)],
        (base, contexts[-1], kept_rows),
        [VM] * 3,
        2 * length * model * group,
    )
    return encoded[None]


def solution(mesh):
    return jax.shard_map(
        body,
        mesh=mesh,
        in_specs=(
            P(("groups", "fsdp"), "ctx", None),
            P(("groups", "fsdp"), "ctx"),
            P(("groups", "fsdp"), "ctx"),
            P(("groups", "fsdp"), "ctx"),
            P(),
            P(),
            P(),
            P("fsdp", None),
            P(None, "fsdp"),
        ),
        out_specs=P(("groups", "fsdp"), "ctx", None),
        check_vma=False,
    )
```
